32 devices in a mesh: groups: 2 (over y), tm: 4 (over z), cuts: 2 (over x), col: 2 (over core).
Axes of the slice: x: 2, y: 2, z: 4, core: 2. Of those that a mesh axis runs over, the one named last changes fastest.
Arguments:
- turns: bfloat16 [4096, 4, 1280], P(('groups', 'tm'), 'cuts', 'col'), parts along dimension 0, may hold values from -25 to 25
- shifts: int32 [8], P(('groups', 'tm')), parts along dimension 0, may hold values from -16 to 16
- bands: int32 [8], P(('groups', 'cuts')), parts along dimension 0, may hold values from 2 to 24
- memory: float32 [8], P(('groups', 'cuts')), parts along dimension 0, may hold values from 0.8 to 0.995
Outputs:
- filtered: bfloat16 [8192, 4, 1280], P(('groups', 'tm', 'col'), 'cuts'), parts along dimension 0
The draws below stay inside these ranges and needn't reach their ends.
There are 2 independent parts, one for each index of `groups`. The reference program is written for one: setup_inputs(seed, part) draws one part's arguments, and reference() takes and returns one part's arrays. A program takes and returns all parts, laid end to end along the dimension named above; each array names one. Nothing has to cross between parts.
All inputs are finite; a program needn't handle non-finite values.
Results may differ from the reference program's by a relative error of at most 0.015.
The reference program's roundings to bfloat16 on the way count: a program that leaves them out, or rounds other values in their place, can miss the bound.
Values may be sent and summed in bfloat16 or wider, within the bound.
No kernel may reach another device: no remote copies, remote signals or barrier semaphores. Data moves between devices by JAX's collectives and lax.ppermute only.
A program may use at most 64 MiB of HBM per device.

```python
import math
import jax
import jax.numpy as jnp
from jax import lax

ANGLES = 1024
COLUMNS = 1280
BAND_FREQS = 64
HALF = 512
SLICES = 4
WINDOWS = 4


def cycle_pattern(base_key, block_count, amp_low, amp_high):
    col_pos = jnp.arange(COLUMNS, dtype=jnp.int32).astype(jnp.float32)
    low_freq = min(28.0, 0.25 * COLUMNS)
    high_freq = min(52.0, 0.5 * COLUMNS)
    pattern = jnp.zeros((block_count, 1, SLICES, COLUMNS), jnp.float32)
    for term_index in range(6):
        term_keys = jax.random.split(jax.random.fold_in(base_key, term_index), 3)
        wave_freq = jax.random.uniform(term_keys[0], (block_count, 1, SLICES, 1), jnp.float32, low_freq, high_freq)
        wave_amp = jax.random.uniform(term_keys[1], (block_count, 1, SLICES, 1), jnp.float32, amp_low, amp_high)
        wave_phase = jax.random.uniform(term_keys[2], (block_count, 1, SLICES, 1), jnp.float32, -math.pi, math.pi)
        pattern = pattern + wave_amp * jnp.cos(col_pos * (2.0 * math.pi / COLUMNS) * wave_freq + wave_phase)
    return pattern


def draw_turns(key, part):
    subkeys = jax.random.split(jax.random.fold_in(key, 17), 9)
    blocks = WINDOWS
    col_pos = jnp.arange(COLUMNS, dtype=jnp.int32).astype(jnp.float32)
    angle_pos = jnp.arange(blocks * HALF, dtype=jnp.int32).astype(jnp.float32).reshape(blocks, HALF, 1, 1)
    turn_phase = angle_pos * (2.0 * math.pi / ANGLES)
    beam_phase = jax.random.uniform(subkeys[6], (), jnp.float32, -math.pi, math.pi)
    beam_shape = 0.9 + 0.1 * jnp.cos(col_pos * (2.0 * math.pi / COLUMNS) + beam_phase)
    height_low = 1.5
    height_high = 3.0
    base_noise = 0.08 * jax.random.truncated_normal(subkeys[0], -3.0, 3.0, (blocks, HALF, SLICES, COLUMNS), jnp.float32)
    lasting = cycle_pattern(subkeys[2], 1, 0.6, 1.2)
    cycle_part = cycle_pattern(subkeys[1], blocks, 0.6, 1.2) + lasting
    offsets = 0.4 * jax.random.truncated_normal(subkeys[8], -2.5, 2.5, (blocks, HALF, SLICES, 1), jnp.float32)
    object_part = jnp.zeros((blocks, HALF, 1, COLUMNS), jnp.float32)
    for blob_index in range(12):
        blob_keys = jax.random.split(jax.random.fold_in(subkeys[3], blob_index), 4)
        radius = COLUMNS * jax.random.uniform(blob_keys[0], (), jnp.float32, 0.05, 0.4)
        breadth = jnp.maximum(COLUMNS * jax.random.uniform(blob_keys[1], (), jnp.float32, 0.0035, 0.008), 0.8)
        start_phase = jax.random.uniform(blob_keys[2], (), jnp.float32, -math.pi, math.pi)
        height = jax.random.uniform(blob_keys[3], (), jnp.float32, height_low, height_high)
        center = 0.5 * COLUMNS + radius * jnp.cos(turn_phase + start_phase)
        distance = (col_pos - center) / breadth
        object_part = object_part + height * jnp.exp(-0.5 * distance * distance)
    full_field = jnp.clip(base_noise + cycle_part + object_part + offsets * beam_shape, -25.0, 25.0)
    return full_field.reshape(blocks * HALF, SLICES, COLUMNS).astype(jnp.bfloat16)


def place_ends(entries, rng, smallest, high):
    spot = [jax.random.randint(jax.random.fold_in(rng, axis), (), 0, length) for axis, length in enumerate(entries.shape)]
    widest = entries.shape.index(max(entries.shape))
    neighbour = spot[:widest] + [(spot[widest] + 1) % entries.shape[widest]] + spot[widest + 1:]
    return entries.at[tuple(spot)].set(smallest).at[tuple(neighbour)].set(high)


def levels(rng, dims, cuts, least, top_value):
    gain, own = 1.0, jax.random.fold_in(rng, 6)
    for position, blocks in cuts:
        draws = jnp.exp(jax.random.uniform(jax.random.fold_in(own, position), (blocks,), jnp.float32, least / len(cuts), top_value / len(cuts)))
        gain = gain * jnp.repeat(draws, dims[position] // blocks).reshape([-1 if axis == position else 1 for axis in range(len(dims))])
    return gain


def setup_inputs(seed: int = 0, part: int = 0) -> dict:
    arg_keys = jax.random.split(jax.random.key(seed), 5)
    part_keys = jax.random.split(jax.random.fold_in(arg_keys[4], part), 5)
    return {
        "turns": draw_turns(jax.random.fold_in(jax.random.fold_in(arg_keys[4], part), 71), part),
        "shifts": place_ends(jax.random.randint(part_keys[1], (WINDOWS,), -16, 17), jax.random.fold_in(part_keys[1], 1), -16, 16).astype(jnp.int32),
        "bands": place_ends(jax.random.randint(part_keys[2], (SLICES,), 2, 25), jax.random.fold_in(part_keys[2], 1), 2, 24).astype(jnp.int32),
        "memory": jnp.clip(jnp.exp(math.log(0.995) - 0.218131 * jax.random.uniform(part_keys[3], (SLICES,), jnp.float32) ** levels(part_keys[3], (SLICES,), ((0, 2),), -0.2, 0.2)), 0.8, 0.995),
    }


def wave_table(angle_count, freq_count):
    freq_index = lax.broadcasted_iota(jnp.int32, (freq_count, angle_count), 0) + 1
    angle_index = lax.broadcasted_iota(jnp.int32, (freq_count, angle_count), 1)
    phase_int = (freq_index * angle_index) % angle_count
    radians = phase_int.astype(jnp.float32) * (2.0 * math.pi / angle_count)
    return jnp.concatenate([jnp.cos(radians), jnp.sin(radians)], axis=0).astype(jnp.bfloat16)


def damping_weights(bands, freq_count, angle_count):
    freq_values = (jnp.arange(freq_count, dtype=jnp.int32) + 1).astype(jnp.float32)
    band_width = bands.astype(jnp.float32)
    gaussian = jnp.exp(-(freq_values[:, None] ** 2) / (2.0 * band_width[None, :] ** 2)) * (2.0 / angle_count)
    return jnp.concatenate([gaussian, gaussian], axis=0)


def ramp_taps(lag_index, width_total):
    distance = jnp.minimum(lag_index, width_total - lag_index)
    dist_float = jnp.maximum(distance, 1).astype(jnp.float32)
    tap_value = jnp.where(distance == 0, 0.25, jnp.where(distance % 2 == 1, -1.0 / (math.pi ** 2 * dist_float ** 2), 0.0))
    return tap_value.astype(jnp.bfloat16)


def reference(turns, shifts, bands, memory):
    wave_rows = wave_table(ANGLES, BAND_FREQS).astype(jnp.float32)
    weights = damping_weights(bands, BAND_FREQS, ANGLES)
    decay_rate = memory[:, None]
    weighted_sum = jnp.zeros((SLICES, COLUMNS), jnp.float32)
    weight = jnp.zeros((SLICES, 1), jnp.float32)
    previous = jnp.zeros((HALF, SLICES, COLUMNS), jnp.bfloat16)
    column_index = jnp.arange(COLUMNS, dtype=jnp.int32)
    outputs = []
    for window_index in range(WINDOWS):
        current = turns[window_index * HALF:(window_index + 1) * HALF]
        window = jnp.concatenate([previous, current], axis=0)
        flat_window = window.reshape(ANGLES, SLICES * COLUMNS).astype(jnp.float32)
        profile = (jnp.sum(flat_window, axis=0) / ANGLES).reshape(SLICES, COLUMNS)
        weighted_sum = decay_rate * weighted_sum + profile
        weight = decay_rate * weight + 1.0
        estimate = weighted_sum / weight
        padded = jnp.pad(estimate, ((1, 1), (0, 0)))
        cycle = (padded[:-2] + 2.0 * padded[1:-1] + padded[2:]) * 0.25
        spectrum = jnp.dot(wave_rows, flat_window, precision=lax.Precision.HIGHEST)
        scaled = (spectrum.reshape(2 * BAND_FREQS, SLICES, COLUMNS) * weights[:, :, None]).astype(jnp.bfloat16)
        low = jnp.dot(wave_rows.T, scaled.reshape(2 * BAND_FREQS, SLICES * COLUMNS).astype(jnp.float32), precision=lax.Precision.HIGHEST)
        damped = (flat_window - low - cycle.reshape(1, SLICES * COLUMNS)).astype(jnp.bfloat16)
        lag_index = (column_index - shifts[window_index]) % COLUMNS
        taps = ramp_taps(lag_index, COLUMNS).astype(jnp.float32)
        rows_in = damped.astype(jnp.float32).reshape(ANGLES, SLICES, COLUMNS)
        result = jnp.fft.irfft(jnp.fft.rfft(rows_in, axis=2) * jnp.fft.rfft(taps), n=COLUMNS, axis=2)
        outputs.append(result.astype(jnp.bfloat16))
        previous = current
    return jnp.concatenate(outputs, axis=0)
```

```python
import functools
import math

import jax
import jax.numpy as jnp
import numpy as np
from jax import lax
from jax.experimental import pallas as pl
from jax.experimental.pallas import tpu as pltpu
from jax.sharding import PartitionSpec as P

BAND_FREQS = 64
WAVES = 2 * BAND_FREQS
TAP_ROWS = 256
PIECES = ((0, 256), (256, 512), (512, 640))

VMEM = pl.BlockSpec(memory_space=pltpu.VMEM)
SMEM = pl.BlockSpec(memory_space=pltpu.SMEM)
F32 = jnp.float32
BF16 = jnp.bfloat16


def signs():
    k = np.arange(WAVES) % BAND_FREQS + 1
    return np.where(k % 2 == 0, 1.0, -1.0).astype(np.float32)


def wave_tables(half, rows):
    k = np.arange(BAND_FREQS)[:, None] + 1
    m = (k * np.arange(half)[None, :]) % (2 * half)
    phase = m.astype(np.float64) * (2.0 * math.pi / (2 * half))
    waves = np.concatenate([np.cos(phase), np.sin(phase)], axis=0).astype(np.float32)
    eye = np.eye(rows, dtype=np.float32)
    spread = (waves[:, None, :, None] * eye[None, :, None, :]).reshape(WAVES * rows, half * rows)
    ones = np.zeros((8, half * rows), np.float32)
    for s in range(rows):
        ones[s, s::rows] = 1.0
    full = np.concatenate([spread, ones], axis=0)
    return full.astype(jnp.bfloat16), np.ascontiguousarray(spread.T).astype(jnp.bfloat16)


def params(flops, size, grant=24 << 20):
    return dict(
        compiler_params=pltpu.CompilerParams(vmem_limit_bytes=grant),
        cost_estimate=pl.CostEstimate(flops=flops, bytes_accessed=size, transcendentals=0),
    )


def split_kernel(raw, table, sign, *outs):
    half, rows, cols = raw.shape
    x = raw[...].reshape(half * rows, cols)
    for (lo, hi), out in zip(PIECES, outs):
        out[...] = x[:, lo:hi]
    outs[-1][...] = sign[...] * jnp.dot(table[...], x, preferred_element_type=F32)


def damp_kernel(owner, lo, q, old, own, spec, table, turned, weights, cycle, keep, send):
    @pl.when(q[0] == owner)
    def _():
        count, cols = old.shape
        waves = turned.shape[1]
        total = jnp.dot(table[:waves, :], old[...], preferred_element_type=F32)
        total = total + spec[:waves, lo : lo + cols]
        ring = cycle[:, lo : lo + cols]
        old_out, own_out = (keep, send) if owner == 0 else (send, keep)
        for half, (source, target) in enumerate(((old, old_out), (own, own_out))):
            scaled = (total * weights[:, half : half + 1]).astype(BF16)
            for r in range(0, count, 256):
                low = jnp.dot(turned[r : r + 256, :], scaled, preferred_element_type=F32)
                left = source[r : r + 256, :].astype(F32) - low
                left = left.reshape(32, 8, cols) - ring[None]
                target[r : r + 256, :] = left.reshape(256, cols).astype(BF16)


def pick(owner, q, keep, recv):
    return jnp.where(q[0] == owner, keep, recv)


def filter_kernel(stages, first, last, rows, q, *refs):
    n = len(stages)
    taps = refs[2 * n]
    acc = None if first else refs[2 * n + 1]
    out = refs[-1]
    width = out.shape[-1]
    step = 256
    count = refs[0].shape[0]

    def block(r):
        total = None if first else acc[r, :]
        for i, (owner, start, cols) in enumerate(stages):
            data = pick(owner, q, refs[2 * i][r, :], refs[2 * i + 1][r, :])
            off = (-start) % width
            part = jnp.dot(data, taps[:cols, off : off + width], preferred_element_type=F32)
            total = part if total is None else total + part
        return total

    if last:
        r = pl.ds(pl.multiple_of(pl.program_id(0) * step, step), step)
        out[...] = block(r).astype(BF16).reshape(step // rows, rows, width)
    else:
        for b in range(0, count, step):
            out[b : b + step, :] = block(slice(b, b + step))


def tap_table(width, shift):
    r = lax.broadcasted_iota(jnp.int32, (TAP_ROWS, 2 * width), 0)
    x = lax.broadcasted_iota(jnp.int32, (TAP_ROWS, 2 * width), 1)
    lag = x - r - shift
    lag = jnp.where(lag < 0, lag + width, lag)
    lag = jnp.where(lag < 0, lag + width, lag)
    lag = jnp.where(lag >= width, lag - width, lag)
    lag = jnp.where(lag >= width, lag - width, lag)
    near = jnp.minimum(lag, width - lag)
    size = jnp.maximum(near, 1).astype(F32)
    tap = jnp.where(near == 0, 0.25, jnp.where(near % 2 == 1, -1.0 / (math.pi**2 * size**2), 0.0))
    return tap.astype(BF16)


def along_tm(x, core, distance):
    tm, cores = lax.axis_size("tm"), lax.axis_size("col")
    route = [(cores * i + core, cores * (i + distance) + core) for i in range(tm - distance)]
    return lax.ppermute(x, ("tm", "col"), route)


def row_neighbours(x):
    cuts, cores = lax.axis_size("cuts"), lax.axis_size("col")
    place = lax.axis_index("cuts")
    last = cores - 1
    if cuts == 1:
        return jnp.zeros_like(x[:1]), jnp.zeros_like(x[:1])
    if cuts == 2:
        edge = jnp.where(place == 0, x[-1:], x[:1])
        got = lax.ppermute(edge, ("cuts", "col"), [(last, cores + last), (cores + last, last)])
        none = jnp.zeros_like(got)
        return jnp.where(place == 0, none, got), jnp.where(place == 0, got, none)
    up = [(cores * i + last, cores * (i + 1) + last) for i in range(cuts - 1)]
    down = [(j, i) for i, j in up]
    before = lax.ppermute(x[-1:], ("cuts", "col"), up)
    after = lax.ppermute(x[:1], ("cuts", "col"), down)
    return before, after


def cycle_of(sums, memory, angles):
    rows, cols = sums.shape
    core = lax.axis_index("col")
    left = lax.ppermute(sums, "col", [(0, 1)])
    whole = jnp.concatenate([left, sums], axis=1)
    decay = memory.reshape(rows, 1)
    older = along_tm(whole, 1, 1)
    window = whole + decay * older
    distance = 2
    while distance < lax.axis_size("tm"):
        got = along_tm(window, 1, distance)
        older = older + decay ** (distance - 1) * got
        window = window + decay**distance * got
        distance *= 2
    total = (whole + decay * older + older) / angles
    steps = lax.axis_index("tm") - jnp.arange(lax.axis_size("tm"), dtype=jnp.int32)
    powers = jnp.power(memory[None, :], jnp.maximum(steps, 0).astype(F32)[:, None])
    weight = jnp.sum(jnp.where(steps[:, None] >= 0, powers, 0.0), axis=0)[:, None]
    estimate = total / weight
    before, after = row_neighbours(estimate)
    padded = jnp.concatenate([before, estimate, after], axis=0)
    smooth = (padded[:-2] + 2.0 * padded[1:-1] + padded[2:]) * 0.25
    given = lax.ppermute(smooth[:, :cols], "col", [(1, 0)])
    return jnp.where(core == 1, smooth[:, cols:], given)


def damping_weights(bands, angles):
    k = (jnp.arange(BAND_FREQS, dtype=jnp.int32) + 1).astype(F32)
    band = bands.astype(F32)
    gaussian = jnp.exp(-(k[:, None] ** 2) / (2.0 * band[None, :] ** 2)) * (2.0 / angles)
    return jnp.concatenate([gaussian, gaussian], axis=0)


def local(turns, shifts, bands, memory):
    half, rows, cols = turns.shape
    angles, count = 2 * half, half * rows
    cores = lax.axis_size("col")
    width = cores * cols
    waves = WAVES * rows
    table, turned = (jnp.asarray(t) for t in wave_tables(half, rows))
    sign = jnp.asarray(np.concatenate([np.repeat(signs(), rows), np.ones(8, np.float32)])[:, None])
    core = lax.axis_index("col").astype(jnp.int32).reshape(1)

    shapes = [jax.ShapeDtypeStruct((count, hi - lo), BF16) for lo, hi in PIECES]
    *pieces, spec = pl.pallas_call(
        split_kernel,
        out_shape=(*shapes, jax.ShapeDtypeStruct((waves + 8, cols), F32)),
        in_specs=[VMEM] * 3,
        out_specs=[VMEM] * (len(PIECES) + 1),
        name="split",
        **params(2 * waves * count * cols, 6 * count * cols),
    )(turns, table, sign)
    olds = {}
    for owner in range(cores):
        for i in range(len(PIECES)):
            olds[owner, i] = along_tm(pieces[i], owner, 1)
    cycle = jnp.tile(cycle_of(spec[waves : waves + rows], memory, angles), (8 // rows, 1))
    gains = damping_weights(bands, angles).reshape(waves, 1)
    gains = jnp.concatenate([gains, gains * sign[:waves]], axis=1)
    taps = tap_table(width, shifts[0])

    def damp(owner, i):
        lo, hi = PIECES[i]
        shape = jax.ShapeDtypeStruct((count, hi - lo), BF16)
        keep, send = pl.pallas_call(
            functools.partial(damp_kernel, owner, lo),
            out_shape=(shape, shape),
            in_specs=[SMEM] + [VMEM] * 7,
            out_specs=[VMEM] * 2,
            name="damp",
            **params(6 * waves * count * (hi - lo), 8 * count * (hi - lo)),
        )(core, olds[owner, i], pieces[i], spec, table, turned, gains, cycle)
        recv = lax.ppermute(send, "col", [(owner, 1 - owner)])
        return (owner, owner * cols + lo, hi - lo), keep, recv

    def accumulate(parts, acc, last):
        stages = tuple(p[0] for p in parts)
        data = [a for p in parts for a in p[1:]]
        inputs = [core, *data, taps] + ([] if acc is None else [acc])
        kernel = functools.partial(filter_kernel, stages, acc is None, last, rows)
        depth = sum(s[2] for s in stages)
        cost = params(2 * count * depth * width, 8 * count * width)
        specs = [SMEM] + [VMEM] * (len(inputs) - 1)
        if last:
            return pl.pallas_call(
                kernel,
                grid=(count // 256,),
                out_shape=jax.ShapeDtypeStruct((half, rows, width), BF16),
                in_specs=specs,
                out_specs=pl.BlockSpec((256 // rows, rows, width), lambda g: (g, 0, 0)),
                name="finish",
                **cost,
            )(*inputs)
        return pl.pallas_call(
            kernel,
            out_shape=jax.ShapeDtypeStruct((count, width), F32),
            in_specs=specs,
            out_specs=VMEM,
            name="accumulate",
            input_output_aliases={} if acc is None else {len(inputs) - 1: 0},
            **cost,
        )(*inputs)

    parts = {key: damp(*key) for key in olds}
    acc = accumulate([parts[0, 0], parts[0, 1]], None, False)
    acc = accumulate([parts[0, 2], parts[1, 0]], acc, False)
    acc = accumulate([parts[1, 1]], acc, False)
    return accumulate([parts[1, 2]], acc, True)


def solution(mesh):
    placed = (
        P(("groups", "tm"), "cuts", "col"),
        P(("groups", "tm")),
        P(("groups", "cuts")),
        P(("groups", "cuts")),
    )
    return jax.shard_map(
        local,
        mesh=mesh,
        in_specs=placed,
        out_specs=P(("groups", "tm", "col"), "cuts", None),
        check_vma=False,
    )
```

```python
import functools
import math

import jax
import jax.numpy as jnp
import numpy as np
from jax import lax
from jax.experimental import pallas as pl
from jax.experimental.pallas import tpu as pltpu
from jax.sharding import PartitionSpec as P

BAND_FREQS = 64
WAVES = 2 * BAND_FREQS
TAP_ROWS = 256
PIECES = ((0, 256), (256, 512), (512, 640))

VMEM = pl.BlockSpec(memory_space=pltpu.VMEM)
SMEM = pl.BlockSpec(memory_space=pltpu.SMEM)
F32 = jnp.float32
BF16 = jnp.bfloat16


def wave_tables(half, rows):
    k = np.arange(BAND_FREQS)[:, None] + 1
    m = (k * np.arange(half)[None, :]) % (2 * half)
    phase = m.astype(np.float64) * (2.0 * math.pi / (2 * half))
    waves = np.concatenate([np.cos(phase), np.sin(phase)], axis=0).astype(np.float32)
    eye = np.eye(rows, dtype=np.float32)
    spread = (waves[:, None, :, None] * eye[None, :, None, :]).reshape(WAVES * rows, half * rows)
    return spread.astype(jnp.bfloat16), np.ascontiguousarray(spread.T).astype(jnp.bfloat16)


def params(flops, size, grant=8 << 20):
    return dict(
        compiler_params=pltpu.CompilerParams(vmem_limit_bytes=grant),
        cost_estimate=pl.CostEstimate(flops=flops, bytes_accessed=size, transcendentals=0),
    )


def pattern(shape, dim, rows):
    return lax.broadcasted_iota(jnp.int32, shape, dim) % rows


def split_kernel(raw, *outs):
    *pieces, sums = outs
    half, rows, cols = raw.shape
    block = 128
    total = None
    for start in range(0, half, block):
        x = raw[start : start + block].reshape(block * rows, cols)
        shape = (8, block * rows)
        pick = pattern(shape, 1, rows) == lax.broadcasted_iota(jnp.int32, shape, 0)
        part = jnp.dot(pick.astype(F32).astype(BF16), x, preferred_element_type=F32)
        total = part if total is None else total + part
        for (lo, hi), out in zip(PIECES, pieces):
            out[start * rows : (start + block) * rows, :] = x[:, lo:hi]
    sums[...] = total[:rows, :]


def spec_kernel(rows, angles, table, bands, *refs):
    *pieces, spec, gain = refs
    waves = spec.shape[0]
    index = lax.broadcasted_iota(jnp.int32, (waves, 1), 0)
    k = index // rows % BAND_FREQS + 1
    flip = jnp.where(k % 2 == 0, 1.0, -1.0)
    for (lo, hi), piece in zip(PIECES, pieces):
        spec[:, lo:hi] = flip * jnp.dot(table[...], piece[...], preferred_element_type=F32)
    band = bands[:, :1]
    for s in range(1, rows):
        band = jnp.where(index % rows == s, bands[:, s : s + 1], band)
    square = (k * k).astype(F32)
    gain[...] = jnp.exp(-square / (2.0 * band * band)) * (2.0 / angles)


def smooth_kernel(estimate, before, after, left, right):
    cols = left.shape[1]
    x = estimate[...]
    place = lax.axis_index("cuts")
    first = jnp.where(place != 0, before[...], 0.0)
    last = jnp.where(place != lax.axis_size("cuts") - 1, after[...], 0.0)
    up = jnp.concatenate([first, x[:-1]], axis=0)
    down = jnp.concatenate([x[1:], last], axis=0)
    ring = (up + 2.0 * x + down) * 0.25
    left[...] = ring[:, :cols]
    right[...] = ring[:, cols:]


def damp_kernel(lo, rows, raw, piece, own, spec, gain, table, turned, left, right, *outs):
    keep, send, old = outs
    count, cols = piece.shape
    waves = turned.shape[1]
    core = lax.axis_index("col")

    @pl.when(core == 0)
    def _():
        old[...] = raw[:, :, lo : lo + cols].reshape(count, cols)

    @pl.when(core != 0)
    def _():
        old[...] = piece[...]

    total = jnp.dot(table[...], old[...], preferred_element_type=F32)
    total = (total + spec[:, lo : lo + cols]) * gain[...]
    index = lax.broadcasted_iota(jnp.int32, (waves, 1), 0)
    k = index // rows % BAND_FREQS + 1
    flip = jnp.where(k % 2 == 0, 1.0, -1.0)
    row = pattern((8, cols), 0, rows)
    ring = None
    for s in range(rows):
        line = jnp.where(
            core == 0, left[s : s + 1, lo : lo + cols], right[s : s + 1, lo : lo + cols]
        )
        line = jnp.broadcast_to(line, (8, cols))
        ring = line if s == 0 else jnp.where(row == s, line, ring)

    def damp(half, source, target):
        scaled = (total if half == 0 else total * flip).astype(BF16)
        for r in range(0, count, 256):
            low = jnp.dot(turned[r : r + 256, :], scaled, preferred_element_type=F32)
            rest = source[r : r + 256, :].astype(F32) - low
            rest = rest.reshape(32, 8, cols) - ring[None]
            target[r : r + 256, :] = rest.reshape(256, cols).astype(BF16)

    @pl.when(core == 0)
    def _():
        damp(1, own, send)
        damp(0, old, keep)

    @pl.when(core != 0)
    def _():
        damp(0, old, send)
        damp(1, own, keep)


def filter_kernel(starts, first, last, rows, *refs):
    n = len(starts)
    taps = refs[n]
    acc = None if first else refs[n + 1]
    out = refs[-1]
    width = out.shape[-1]
    step = 256
    count = refs[0].shape[0]

    def block(r):
        total = None if first else acc[r, :]
        for start, ref in zip(starts, refs):
            off = (-start) % width
            weights = taps[: ref.shape[1], off : off + width]
            part = jnp.dot(ref[r, :], weights, preferred_element_type=F32)
            total = part if total is None else total + part
        return total

    if last:
        r = pl.ds(pl.multiple_of(pl.program_id(0) * step, step), step)
        out[...] = block(r).astype(BF16).reshape(step // rows, rows, width)
    else:
        for b in range(0, count, step):
            out[b : b + step, :] = block(slice(b, b + step))


def tap_kernel(shift, out):
    width = out.shape[1] // 2
    lanes = 128
    for r in range(0, lanes, 16):
        row = lax.broadcasted_iota(jnp.int32, (16, width), 0) + r
        col = lax.broadcasted_iota(jnp.int32, (16, width), 1)
        lag = col - row - shift[0]
        lag = jnp.where(lag < 0, lag + width, lag)
        lag = jnp.where(lag < 0, lag + width, lag)
        near = jnp.minimum(lag, width - lag)
        size = jnp.maximum(near, 1).astype(F32)
        odd = -1.0 / (math.pi**2 * size**2)
        tap = jnp.where(near == 0, 0.25, jnp.where((near & 1) == 1, odd, 0.0)).astype(BF16)
        for b in range(out.shape[0] // lanes):
            for c in range(0, 2 * width, width):
                start = (c + b * lanes) % (2 * width)
                rows = slice(b * lanes + r, b * lanes + r + 16)
                room = min(width, 2 * width - start)
                out[rows, start : start + room] = tap[:, :room]
                if room < width:
                    out[rows, : width - room] = tap[:, room:]


def along_tm(x, core, distance):
    tm, cores = lax.axis_size("tm"), lax.axis_size("col")
    route = [(cores * i + core, cores * (i + distance) + core) for i in range(tm - distance)]
    return lax.ppermute(x, ("tm", "col"), route)


def tiny(body, shapes, *args):
    def kernel(*refs):
        for ref, value in zip(refs[len(args) :], body(*(r[...] for r in refs[: len(args)]))):
            ref[...] = value

    return pl.pallas_call(
        kernel,
        out_shape=tuple(jax.ShapeDtypeStruct(s, F32) for s in shapes),
        in_specs=[VMEM] * len(args),
        out_specs=(VMEM,) * len(shapes),
        **params(1 << 16, 1 << 16),
    )(*args)


def row_edges(x):
    place = lax.axis_index("cuts")
    if lax.axis_size("cuts") == 2:
        return (jnp.where(place == 0, x[-1:], x[:1]),) * 2
    return x[-1:], x[:1]


def row_neighbours(last, first):
    cuts, cores = lax.axis_size("cuts"), lax.axis_size("col")
    at = [cores * i + cores - 1 for i in range(cuts)]
    if cuts == 1:
        return first, last
    if cuts == 2:
        got = lax.ppermute(last, ("cuts", "col"), [(at[0], at[1]), (at[1], at[0])])
        return got, got
    up = list(zip(at[:-1], at[1:]))
    before = lax.ppermute(last, ("cuts", "col"), up)
    after = lax.ppermute(first, ("cuts", "col"), [(j, i) for i, j in up])
    return before, after


def cycle_of(sums, memory, angles):
    rows, cols = sums.shape
    tm, cores = lax.axis_size("tm"), lax.axis_size("col")
    wide = (rows, cores * cols)
    decay = memory.reshape(rows, 1)
    steps = lax.axis_index("tm") - jnp.arange(tm, dtype=jnp.int32)
    powers = jnp.power(memory[None, :], jnp.maximum(steps, 0).astype(F32)[:, None])
    weight = jnp.sum(jnp.where(steps[:, None] >= 0, powers, 0.0), axis=0)[:, None]
    distances = [1 << i for i in range(max(tm - 1, 1).bit_length())]
    scales = [decay ** (d - 1) for d in distances] + [decay**d for d in distances]
    scales = jnp.concatenate(scales + [decay, weight * angles], axis=1)
    n = len(distances)
    left = lax.ppermute(sums, "col", [(0, 1)])
    (whole,) = tiny(lambda a, b: (jnp.concatenate([a, b], axis=1),), [wide], left, sums)
    older, window = None, whole
    for i, d in enumerate(distances):
        got = along_tm(window, 1, d)
        if i == n - 1:
            break

        def extend(c, got, window, older=None, i=i):
            further = got if older is None else older + c[:, i : i + 1] * got
            return further, window + c[:, n + i : n + i + 1] * got

        extra = () if older is None else (older,)
        older, window = tiny(extend, [wide] * 2, scales, got, window, *extra)

    def estimate_of(c, got, whole, older=None):
        total = got if older is None else older + c[:, n - 1 : n] * got
        x = (whole + c[:, 2 * n : 2 * n + 1] * total + total) / c[:, 2 * n + 1 :]
        return x, *row_edges(x)

    extra = () if older is None else (older,)
    edge = (1, wide[1])
    estimate, last, first = tiny(estimate_of, [wide, edge, edge], scales, got, whole, *extra)
    before, after = row_neighbours(last, first)
    shape = jax.ShapeDtypeStruct((rows, cols), F32)
    left, right = pl.pallas_call(
        smooth_kernel,
        out_shape=(shape, shape),
        in_specs=[VMEM] * 3,
        out_specs=[VMEM] * 2,
        name="smooth",
        **params(1 << 16, 1 << 16),
    )(estimate, before, after)
    left = lax.ppermute(left, "col", [(1, 0)])
    return left, right


def local(turns, shifts, bands, memory):
    half, rows, cols = turns.shape
    angles, count = 2 * half, half * rows
    width = lax.axis_size("col") * cols
    waves = WAVES * rows
    table, turned = (jnp.asarray(t) for t in wave_tables(half, rows))
    core = lax.axis_index("col").astype(jnp.int32)

    raw = along_tm(turns, 0, 1)
    shapes = [jax.ShapeDtypeStruct((count, hi - lo), BF16) for lo, hi in PIECES]
    *pieces, sums = pl.pallas_call(
        split_kernel,
        out_shape=(*shapes, jax.ShapeDtypeStruct((rows, cols), F32)),
        in_specs=[VMEM],
        out_specs=[VMEM] * (len(PIECES) + 1),
        name="split",
        **params(16 * count * cols, 4 * count * cols),
    )(turns)
    left, right = cycle_of(sums, memory, angles)
    spec, gain = pl.pallas_call(
        functools.partial(spec_kernel, rows, angles),
        out_shape=(
            jax.ShapeDtypeStruct((waves, cols), F32),
            jax.ShapeDtypeStruct((waves, 1), F32),
        ),
        in_specs=[VMEM] * (2 + len(PIECES)),
        out_specs=[VMEM] * 2,
        name="spec",
        **params(2 * waves * count * cols, 4 * count * cols),
    )(table, bands.astype(F32).reshape(1, rows), *pieces)
    olds = []
    for x in pieces:
        olds.append(along_tm(x, 1, 1))
    offset = (shifts + core.reshape(1) * cols) % width
    taps = pl.pallas_call(
        tap_kernel,
        out_shape=jax.ShapeDtypeStruct((TAP_ROWS, 2 * width), BF16),
        in_specs=[SMEM],
        out_specs=VMEM,
        name="taps",
        **params(1 << 20, 1 << 20),
    )(offset)

    def damp(i):
        lo, hi = PIECES[i]
        shape = jax.ShapeDtypeStruct((count, hi - lo), BF16)
        keep, send = pl.pallas_call(
            functools.partial(damp_kernel, lo, rows),
            out_shape=(shape, shape),
            in_specs=[VMEM] * 9,
            out_specs=[VMEM] * 2,
            scratch_shapes=[pltpu.VMEM((count, hi - lo), BF16)],
            **params(6 * waves * count * (hi - lo), 8 * count * (hi - lo)),
        )(raw, olds[i], pieces[i], spec, gain, table, turned, left, right)
        recv = lax.ppermute(send, "col", [(0, 1), (1, 0)])
        return (lo, cols + lo), (keep, recv)

    def accumulate(part, acc, last):
        starts, data = part
        inputs = [*data, taps] + ([] if acc is None else [acc])
        kernel = functools.partial(filter_kernel, starts, acc is None, last, rows)
        depth = 2 * data[0].shape[1]
        cost = params(2 * count * depth * width, 8 * count * width)
        specs = [VMEM] * len(inputs)
        if last:
            return pl.pallas_call(
                kernel,
                grid=(count // 256,),
                out_shape=jax.ShapeDtypeStruct((half, rows, width), BF16),
                in_specs=specs,
                out_specs=pl.BlockSpec((256 // rows, rows, width), lambda g: (g, 0, 0)),
                name="finish",
                **cost,
            )(*inputs)
        return pl.pallas_call(
            kernel,
            out_shape=jax.ShapeDtypeStruct((count, width), F32),
            in_specs=specs,
            out_specs=VMEM,
            input_output_aliases={} if acc is None else {len(inputs) - 1: 0},
            **cost,
        )(*inputs)

    acc = None
    for i in range(len(PIECES)):
        acc = accumulate(damp(i), acc, i == len(PIECES) - 1)
    return acc


def solution(mesh):
    placed = (
        P(("groups", "tm"), "cuts", "col"),
        P(("groups", "tm")),
        P(("groups", "cuts")),
        P(("groups", "cuts")),
    )

    return jax.shard_map(
        local,
        mesh=mesh,
        in_specs=placed,
        out_specs=P(("groups", "tm", "col"), "cuts", None),
        check_vma=False,
    )
```

```python
import functools
import math

import jax
import jax.numpy as jnp
import numpy as np
from jax import lax
from jax.experimental import pallas as pl
from jax.experimental.pallas import tpu as pltpu
from jax.sharding import PartitionSpec as P

BAND_FREQS = 64
WAVES = 2 * BAND_FREQS
TAP_ROWS = 256
PIECES = ((0, 128), (128, 256), (256, 512), (512, 640))
GROUPS = ((0, 1), (2,), (3,))
WRAPS = 2

VMEM = pl.BlockSpec(memory_space=pltpu.VMEM)
SMEM = pl.BlockSpec(memory_space=pltpu.SMEM)
HBM = pl.BlockSpec(memory_space=pltpu.HBM)
F32 = jnp.float32
BF16 = jnp.bfloat16


def wave_tables(half, rows):
    k = np.arange(BAND_FREQS)[:, None] + 1
    m = (k * np.arange(half)[None, :]) % (2 * half)
    phase = m.astype(np.float64) * (2.0 * math.pi / (2 * half))
    waves = np.concatenate([np.cos(phase), np.sin(phase)], axis=0).astype(np.float32)
    eye = np.eye(rows, dtype=np.float32)
    spread = (waves[:, None, :, None] * eye[None, :, None, :]).reshape(WAVES * rows, half * rows)
    return spread.astype(jnp.bfloat16), np.ascontiguousarray(spread.T).astype(jnp.bfloat16)


def params(flops, size, grant=8 << 20):
    return dict(
        compiler_params=pltpu.CompilerParams(vmem_limit_bytes=grant),
        cost_estimate=pl.CostEstimate(flops=flops, bytes_accessed=size, transcendentals=0),
    )


def pattern(shape, dim, rows):
    return lax.broadcasted_iota(jnp.int32, shape, dim) % rows


def split_kernel(raw, *refs):
    *pieces, sums = refs
    half, rows, cols = raw.shape
    x = raw[...].reshape(half * rows, cols)
    for (lo, hi), out in zip(PIECES, pieces):
        out[...] = x[:, lo:hi]
    shape = (8, half * rows)
    pick = pattern(shape, 1, rows) == lax.broadcasted_iota(jnp.int32, shape, 0)
    total = jnp.dot(pick.astype(F32).astype(BF16), x, preferred_element_type=F32)
    sums[...] = total[:rows, :]


def spec_kernel(rows, distances, angles, bands, memory, table, *refs):
    *pieces, spec, gain, scales = refs
    waves = spec.shape[0]
    index = lax.broadcasted_iota(jnp.int32, (waves, 1), 0)
    k = index // rows % BAND_FREQS + 1
    flip = jnp.where(k % 2 == 0, 1.0, -1.0)
    for (lo, hi), piece in zip(PIECES, pieces):
        spec[:, lo:hi] = flip * jnp.dot(table[...], piece[...], preferred_element_type=F32)
    band = jnp.full((waves, 1), bands[0], jnp.int32)
    row = lax.broadcasted_iota(jnp.int32, (rows, 1), 0)
    decay = jnp.full((rows, 1), memory[0], F32)
    for s in range(1, rows):
        band = jnp.where(index % rows == s, bands[s], band)
        decay = jnp.where(row == s, memory[s], decay)
    square = (k * k).astype(F32)
    gain[...] = jnp.exp(-square / (2.0 * (band * band).astype(F32))) * (2.0 / angles)
    power, done = decay, 1
    for i, d in enumerate(distances):
        while done < d:
            power, done = power * power, 2 * done
        scales[:, i : i + 1] = jnp.ones_like(decay) if d == 1 else power / decay
        scales[:, len(distances) + i : len(distances) + i + 1] = power
    weight = jnp.ones_like(decay)
    steps = lax.axis_index("tm")
    for j in range(lax.axis_size("tm") - 1):
        weight = jnp.where(j < steps, weight * decay + 1.0, weight)
    scales[:, 2 * len(distances) : 2 * len(distances) + 1] = decay
    scales[:, 2 * len(distances) + 1 : 2 * len(distances) + 2] = 1.0 / (weight * angles)


def smooth_kernel(estimate, before, after, out):
    rows, cols = estimate.shape
    x = estimate[...]
    place = lax.axis_index("cuts")
    first = jnp.where(place != 0, before[...], 0.0)
    last = jnp.where(place != lax.axis_size("cuts") - 1, after[...], 0.0)
    up = jnp.concatenate([first, x[:-1]], axis=0)
    down = jnp.concatenate([x[1:], last], axis=0)
    ring = (up + 2.0 * x + down) * 0.25
    row = pattern((8, cols), 0, rows)
    total = jnp.broadcast_to(ring[:1], (8, cols))
    for s in range(1, rows):
        total = jnp.where(row == s, jnp.broadcast_to(ring[s : s + 1], (8, cols)), total)
    out[...] = total


def damp_kernel(lo, rows, piece, own, spec, gain, table, turned, cycle, keep, send, old):
    count, cols = piece.shape
    waves = turned.shape[1]
    core = lax.axis_index("col")
    old[...] = jnp.where(lax.axis_index("tm") > 0, piece[...], jnp.zeros_like(piece))
    total = jnp.dot(table[...], old[...], preferred_element_type=F32)
    total = (total + spec[:, lo : lo + cols]) * gain[...]
    index = lax.broadcasted_iota(jnp.int32, (waves, 1), 0)
    k = index // rows % BAND_FREQS + 1
    flip = jnp.where(k % 2 == 0, 1.0, -1.0)
    ring = cycle[:, lo : lo + cols]

    def damp(half, source, target):
        scaled = (total if half == 0 else total * flip).astype(BF16)
        for r in range(0, count, 256):
            low = jnp.dot(turned[r : r + 256, :], scaled, preferred_element_type=F32)
            rest = source[r : r + 256, :].astype(F32) - low
            rest = rest.reshape(32, 8, cols) - ring[None]
            target[r : r + 256, :] = rest.reshape(256, cols).astype(BF16)

    @pl.when(core == 0)
    def _():
        damp(1, own, send)
        damp(0, old, keep)

    @pl.when(core != 0)
    def _():
        damp(0, old, send)
        damp(1, own, keep)


def filter_kernel(starts, first, last, rows, *refs):
    n = len(starts)
    taps = refs[n]
    acc = None if first else refs[n + 1]
    out = refs[-1]
    width = out.shape[-1]
    step = 256
    count = refs[0].shape[0]

    def block(r):
        total = None if first else acc[r, :]
        for start, ref in zip(starts, refs):
            off = (-start) % width
            weights = taps[: ref.shape[1], off : off + width]
            part = jnp.dot(ref[r, :], weights, preferred_element_type=F32)
            total = part if total is None else total + part
        return total

    if last:
        r = pl.ds(pl.multiple_of(pl.program_id(0) * step, step), step)
        out[...] = block(r).astype(BF16).reshape(step // rows, rows, width)
    else:
        for b in range(0, count, step):
            out[b : b + step, :] = block(slice(b, b + step))


def tap_kernel(shift, out):
    width = out.shape[1] // 2
    lanes = 128
    for r in range(0, lanes, 16):
        row = lax.broadcasted_iota(jnp.int32, (16, width), 0) + r
        col = lax.broadcasted_iota(jnp.int32, (16, width), 1)
        lag = col - row - shift[0]
        lag = jnp.where(lag < 0, lag + width, lag)
        lag = jnp.where(lag < 0, lag + width, lag)
        near = jnp.minimum(lag, width - lag)
        size = jnp.maximum(near, 1).astype(F32)
        odd = -1.0 / (math.pi**2 * size**2)
        tap = jnp.where(near == 0, 0.25, jnp.where((near & 1) == 1, odd, 0.0)).astype(BF16)
        for b in range(out.shape[0] // lanes):
            for c in range(0, 2 * width, width):
                start = (c + b * lanes) % (2 * width)
                rows = slice(b * lanes + r, b * lanes + r + 16)
                room = min(width, 2 * width - start)
                out[rows, start : start + room] = tap[:, :room]
                if room < width:
                    out[rows, : width - room] = tap[:, room:]


def along_tm(x, distance, wrap=True):
    tm = lax.axis_size("tm")
    route = [(i, (i + distance) % tm) for i in range(tm if wrap else tm - distance)]
    return lax.ppermute(x, "tm", route)


def tiny(body, shapes, *args):
    def kernel(*refs):
        for ref, value in zip(refs[len(args) :], body(*(r[...] for r in refs[: len(args)]))):
            ref[...] = value

    return pl.pallas_call(
        kernel,
        out_shape=tuple(jax.ShapeDtypeStruct(s, F32) for s in shapes),
        in_specs=[VMEM] * len(args),
        out_specs=(VMEM,) * len(shapes),
        **params(1 << 16, 1 << 16),
    )(*args)


def row_edges(x):
    place = lax.axis_index("cuts")
    if lax.axis_size("cuts") == 2:
        return (jnp.where(place == 0, x[-1:], x[:1]),) * 2
    return x[-1:], x[:1]


def row_neighbours(last, first):
    cuts = lax.axis_size("cuts")
    if cuts == 1:
        return first, last
    up = [(i, (i + 1) % cuts) for i in range(cuts)]
    before = lax.ppermute(last, "cuts", up)
    if cuts == 2:
        return before, before
    return before, lax.ppermute(first, "cuts", [(j, i) for i, j in up])


def lag_distances(tm):
    return [1 << i for i in range(max(tm - 1, 1).bit_length())]


def cycle_of(sums, first_lag, scales):
    rows, cols = sums.shape
    wide = (rows, cols)
    distances = lag_distances(lax.axis_size("tm"))
    n = len(distances)
    older, window, got = None, sums, first_lag
    for i, d in enumerate(distances):
        if i > 0:
            got = along_tm(window, d)
        if i == n - 1:
            break

        def extend(c, got, window, older=None, i=i, d=d):
            got = jnp.where(lax.axis_index("tm") >= d, got, 0.0)
            further = got if older is None else older + c[:, i : i + 1] * got
            return further, window + c[:, n + i : n + i + 1] * got

        extra = () if older is None else (older,)
        older, window = tiny(extend, [wide] * 2, scales, got, window, *extra)

    def estimate_of(c, got, whole, older=None):
        got = jnp.where(lax.axis_index("tm") >= distances[-1], got, 0.0)
        total = got if older is None else older + c[:, n - 1 : n] * got
        total = whole + c[:, 2 * n : 2 * n + 1] * total + total
        x = total * c[:, 2 * n + 1 : 2 * n + 2]
        return x, *row_edges(x)

    extra = () if older is None else (older,)
    edge = (1, cols)
    estimate, last, first = tiny(estimate_of, [wide, edge, edge], scales, got, sums, *extra)
    before, after = row_neighbours(last, first)
    return pl.pallas_call(
        smooth_kernel,
        out_shape=jax.ShapeDtypeStruct((8, cols), F32),
        in_specs=[VMEM] * 3,
        out_specs=VMEM,
        name="smooth",
        **params(1 << 16, 1 << 16),
    )(estimate, before, after)


def local(turns, shifts, bands, memory):
    half, rows, cols = turns.shape
    angles, count = 2 * half, half * rows
    width = lax.axis_size("col") * cols
    waves = WAVES * rows
    table, turned = (jnp.asarray(t) for t in wave_tables(half, rows))
    core = lax.axis_index("col").astype(jnp.int32)
    distances = lag_distances(lax.axis_size("tm"))
    n = len(PIECES)

    shapes = [jax.ShapeDtypeStruct((count, hi - lo), BF16) for lo, hi in PIECES]
    *pieces, sums = pl.pallas_call(
        split_kernel,
        out_shape=(*shapes, jax.ShapeDtypeStruct((rows, cols), F32)),
        in_specs=[VMEM],
        out_specs=[VMEM] * (n + 1),
        name="split",
        **params(16 * count * cols, 4 * count * cols),
    )(turns)
    spec, gain, scales = pl.pallas_call(
        functools.partial(spec_kernel, rows, distances, angles),
        out_shape=(
            jax.ShapeDtypeStruct((waves, cols), F32),
            jax.ShapeDtypeStruct((waves, 1), F32),
            jax.ShapeDtypeStruct((rows, 128), F32),
        ),
        in_specs=[SMEM] * 2 + [VMEM] * (1 + n),
        out_specs=[VMEM] * 3,
        name="spec",
        **params(2 * waves * count * cols, 4 * count * cols),
    )(bands, memory, table, *pieces)
    first_lag = along_tm(sums, 1)
    cycle = cycle_of(sums, first_lag, scales)
    olds = []
    for i, x in enumerate(pieces):
        olds.append(along_tm(x, 1, wrap=i < WRAPS))
    offset = (shifts + core.reshape(1) * cols) % width
    taps = pl.pallas_call(
        tap_kernel,
        out_shape=jax.ShapeDtypeStruct((TAP_ROWS, 2 * width), BF16),
        in_specs=[SMEM],
        out_specs=VMEM,
        name="taps",
        **params(1 << 20, 1 << 20),
    )(offset)

    def damp(i):
        lo, hi = PIECES[i]
        shape = jax.ShapeDtypeStruct((count, hi - lo), BF16)
        keep, send = pl.pallas_call(
            functools.partial(damp_kernel, lo, rows),
            out_shape=(shape, shape),
            in_specs=[VMEM] * 7,
            out_specs=[VMEM] * 2,
            scratch_shapes=[pltpu.VMEM((count, hi - lo), BF16)],
            **params(6 * waves * count * (hi - lo), 8 * count * (hi - lo)),
        )(olds[i], pieces[i], spec, gain, table, turned, cycle)
        recv = lax.ppermute(send, "col", [(0, 1), (1, 0)])
        return (lo, cols + lo), (keep, recv)

    def accumulate(parts, acc, last):
        starts = sum((p[0] for p in parts), ())
        data = sum((p[1] for p in parts), ())
        inputs = [*data, taps] + ([] if acc is None else [acc])
        kernel = functools.partial(filter_kernel, starts, acc is None, last, rows)
        depth = sum(x.shape[1] for x in data)
        cost = params(2 * count * depth * width, 8 * count * width)
        specs = [VMEM] * len(inputs)
        if last:
            return pl.pallas_call(
                kernel,
                grid=(count // 256,),
                out_shape=jax.ShapeDtypeStruct((half, rows, width), BF16),
                in_specs=specs,
                out_specs=pl.BlockSpec((256 // rows, rows, width), lambda g: (g, 0, 0)),
                name="finish",
                **cost,
            )(*inputs)
        return pl.pallas_call(
            kernel,
            out_shape=jax.ShapeDtypeStruct((count, width), F32),
            in_specs=specs,
            out_specs=VMEM,
            input_output_aliases={} if acc is None else {len(inputs) - 1: 0},
            **cost,
        )(*inputs)

    parts = [damp(i) for i in range(n)]
    acc = None
    for i, group in enumerate(GROUPS):
        acc = accumulate([parts[j] for j in group], acc, i == len(GROUPS) - 1)
    return acc


def solution(mesh):
    placed = (
        P(("groups", "tm"), "cuts", "col"),
        P(("groups", "tm")),
        P(("groups", "cuts")),
        P(("groups", "cuts")),
    )

    return jax.shard_map(
        local,
        mesh=mesh,
        in_specs=placed,
        out_specs=P(("groups", "tm", "col"), "cuts", None),
        check_vma=False,
    )
```

```python
import functools
import math

import jax
import jax.numpy as jnp
import numpy as np
from jax import lax
from jax.experimental import pallas as pl
from jax.experimental.pallas import tpu as pltpu
from jax.sharding import PartitionSpec as P

BAND_FREQS = 64
WAVES = 2 * BAND_FREQS
TAP_ROWS = 256
PIECES = ((0, 128), (128, 256), (256, 512), (512, 640))
STAGES = ((0, 1), (2,), (3,))
WRAPS = (0, 1)

VMEM = pl.BlockSpec(memory_space=pltpu.VMEM)
SMEM = pl.BlockSpec(memory_space=pltpu.SMEM)
ANY = pl.BlockSpec(memory_space=pl.ANY)
F32 = jnp.float32
BF16 = jnp.bfloat16


def wave_tables(half, rows):
    k = np.arange(BAND_FREQS)[:, None] + 1
    m = (k * np.arange(half)[None, :]) % (2 * half)
    phase = m.astype(np.float64) * (2.0 * math.pi / (2 * half))
    waves = np.concatenate([np.cos(phase), np.sin(phase)], axis=0).astype(np.float32)
    eye = np.eye(rows, dtype=np.float32)
    spread = (waves[:, None, :, None] * eye[None, :, None, :]).reshape(WAVES * rows, half * rows)
    return spread.astype(jnp.bfloat16), np.ascontiguousarray(spread.T).astype(jnp.bfloat16)


def params(flops, size, grant=8 << 20):
    return dict(
        compiler_params=pltpu.CompilerParams(vmem_limit_bytes=grant),
        cost_estimate=pl.CostEstimate(flops=flops, bytes_accessed=size, transcendentals=0),
    )


def pattern(shape, dim, rows):
    return lax.broadcasted_iota(jnp.int32, shape, dim) % rows


def fetch(raw, buffer, sems, columns):
    count = sems.shape[0]
    block = raw.shape[0] // count
    parts = [pl.ds(i * block, block) for i in range(count)]
    copies = [
        pltpu.make_async_copy(raw.at[p, :, columns], buffer.at[p], sems.at[i])
        for i, p in enumerate(parts)
    ]
    for copy in copies:
        copy.start()
    return copies


def head_kernel(raw, out, buffer, sems):
    half, rows, cols = buffer.shape
    block = half // sems.shape[0]
    for i, copy in enumerate(fetch(raw, buffer, sems, pl.ds(*PIECES[0]))):
        copy.wait()
        x = buffer[i * block : (i + 1) * block].reshape(block * rows, cols)
        out[i * block * rows : (i + 1) * block * rows, :] = x


def split_kernel(raw, *refs):
    *pieces, sums, buffer, sems = refs
    half, rows, cols = buffer.shape
    block = half // sems.shape[0]
    shape = (8, block * rows)
    pick = pattern(shape, 1, rows) == lax.broadcasted_iota(jnp.int32, shape, 0)
    pick = pick.astype(F32).astype(BF16)
    total = None
    for i, copy in enumerate(fetch(raw, buffer, sems, pl.ds(0, cols))):
        copy.wait()
        x = buffer[i * block : (i + 1) * block].reshape(block * rows, cols)
        for (lo, hi), out in zip(PIECES[1:], pieces):
            out[i * block * rows : (i + 1) * block * rows, :] = x[:, lo:hi]
        part = jnp.dot(pick, x, preferred_element_type=F32)
        total = part if total is None else total + part
    sums[...] = total[:rows, :]


def spec_kernel(rows, distances, angles, bands, memory, table, *refs):
    *pieces, spec, gain, scales = refs
    waves = spec.shape[0]
    index = lax.broadcasted_iota(jnp.int32, (waves, 1), 0)
    k = index // rows % BAND_FREQS + 1
    flip = jnp.where(k % 2 == 0, 1.0, -1.0)
    for (lo, hi), piece in zip(PIECES, pieces):
        spec[:, lo:hi] = flip * jnp.dot(table[...], piece[...], preferred_element_type=F32)
    band = jnp.full((waves, 1), bands[0], jnp.int32)
    row = lax.broadcasted_iota(jnp.int32, (rows, 1), 0)
    decay = jnp.full((rows, 1), memory[0], F32)
    for s in range(1, rows):
        band = jnp.where(index % rows == s, bands[s], band)
        decay = jnp.where(row == s, memory[s], decay)
    square = (k * k).astype(F32)
    gain[...] = jnp.exp(-square / (2.0 * (band * band).astype(F32))) * (2.0 / angles)
    power, done = decay, 1
    for i, d in enumerate(distances):
        while done < d:
            power, done = power * power, 2 * done
        scales[:, i : i + 1] = jnp.ones_like(decay) if d == 1 else power / decay
        scales[:, len(distances) + i : len(distances) + i + 1] = power
    weight = jnp.ones_like(decay)
    steps = lax.axis_index("tm")
    for j in range(lax.axis_size("tm") - 1):
        weight = jnp.where(j < steps, weight * decay + 1.0, weight)
    scales[:, 2 * len(distances) : 2 * len(distances) + 1] = decay
    scales[:, 2 * len(distances) + 1 : 2 * len(distances) + 2] = 1.0 / (weight * angles)


def smooth_kernel(estimate, before, after, out):
    rows, cols = estimate.shape
    x = estimate[...]
    place = lax.axis_index("cuts")
    first = jnp.where(place != 0, before[...], 0.0)
    last = jnp.where(place != lax.axis_size("cuts") - 1, after[...], 0.0)
    up = jnp.concatenate([first, x[:-1]], axis=0)
    down = jnp.concatenate([x[1:], last], axis=0)
    ring = (up + 2.0 * x + down) * 0.25
    row = pattern((8, cols), 0, rows)
    total = jnp.broadcast_to(ring[:1], (8, cols))
    for s in range(1, rows):
        total = jnp.where(row == s, jnp.broadcast_to(ring[s : s + 1], (8, cols)), total)
    out[...] = total


def damp_kernel(lo, rows, parts, *refs):
    pieces, owns = refs[:parts], refs[parts : 2 * parts]
    spec, gain, table, turned, cycle, keep, send, old, own = refs[2 * parts :]
    count, cols = old.shape
    waves = turned.shape[1]
    core = lax.axis_index("col")
    at = 0
    for piece, mine in zip(pieces, owns):
        place = slice(at, at + piece.shape[1])
        at = place.stop
        older = piece[...]
        old[:, place] = jnp.where(lax.axis_index("tm") > 0, older, jnp.zeros_like(older))
        if parts > 1:
            own[:, place] = mine[...]
    if parts == 1:
        own = owns[0]
    total = jnp.dot(table[...], old[...], preferred_element_type=F32)
    total = (total + spec[:, lo : lo + cols]) * gain[...]
    index = lax.broadcasted_iota(jnp.int32, (waves, 1), 0)
    k = index // rows % BAND_FREQS + 1
    flip = jnp.where(k % 2 == 0, 1.0, -1.0)
    ring = cycle[:, lo : lo + cols]

    def damp(half, source, target):
        scaled = (total if half == 0 else total * flip).astype(BF16)
        for r in range(0, count, 256):
            low = jnp.dot(turned[r : r + 256, :], scaled, preferred_element_type=F32)
            rest = source[r : r + 256, :].astype(F32) - low
            rest = rest.reshape(32, 8, cols) - ring[None]
            target[r : r + 256, :] = rest.reshape(256, cols).astype(BF16)

    @pl.when(core == 0)
    def _():
        damp(1, own, send)
        damp(0, old, keep)

    @pl.when(core != 0)
    def _():
        damp(0, old, send)
        damp(1, own, keep)


def filter_kernel(starts, first, last, rows, *refs):
    n = len(starts)
    taps = refs[n]
    acc = None if first else refs[n + 1]
    out = refs[-1]
    width = out.shape[-1]
    step = 256
    count = refs[0].shape[0]

    def block(r):
        total = None if first else acc[r, :]
        for start, ref in zip(starts, refs):
            off = (-start) % width
            weights = taps[: ref.shape[1], off : off + width]
            part = jnp.dot(ref[r, :], weights, preferred_element_type=F32)
            total = part if total is None else total + part
        return total

    if last:
        r = pl.ds(pl.multiple_of(pl.program_id(0) * step, step), step)
        out[...] = block(r).astype(BF16).reshape(step // rows, rows, width)
    else:
        for b in range(0, count, step):
            out[b : b + step, :] = block(slice(b, b + step))


def tap_kernel(shift, out):
    width = out.shape[1] // 2
    lanes = 128
    for r in range(0, lanes, 16):
        row = lax.broadcasted_iota(jnp.int32, (16, width), 0) + r
        col = lax.broadcasted_iota(jnp.int32, (16, width), 1)
        lag = col - row - shift[0]
        lag = jnp.where(lag < 0, lag + width, lag)
        lag = jnp.where(lag < 0, lag + width, lag)
        near = jnp.minimum(lag, width - lag)
        size = jnp.maximum(near, 1).astype(F32)
        odd = -1.0 / (math.pi**2 * size**2)
        tap = jnp.where(near == 0, 0.25, jnp.where((near & 1) == 1, odd, 0.0)).astype(BF16)
        for b in range(out.shape[0] // lanes):
            for c in range(0, 2 * width, width):
                start = (c + b * lanes) % (2 * width)
                rows = slice(b * lanes + r, b * lanes + r + 16)
                room = min(width, 2 * width - start)
                out[rows, start : start + room] = tap[:, :room]
                if room < width:
                    out[rows, : width - room] = tap[:, room:]


def along_tm(x, distance, wrap=True):
    tm = lax.axis_size("tm")
    route = [(i, (i + distance) % tm) for i in range(tm if wrap else tm - distance)]
    return lax.ppermute(x, "tm", route)


def tiny(body, shapes, *args):
    def kernel(*refs):
        for ref, value in zip(refs[len(args) :], body(*(r[...] for r in refs[: len(args)]))):
            ref[...] = value

    return pl.pallas_call(
        kernel,
        out_shape=tuple(jax.ShapeDtypeStruct(s, F32) for s in shapes),
        in_specs=[VMEM] * len(args),
        out_specs=(VMEM,) * len(shapes),
        **params(1 << 16, 1 << 16),
    )(*args)


def row_edges(x):
    place = lax.axis_index("cuts")
    if lax.axis_size("cuts") == 2:
        return (jnp.where(place == 0, x[-1:], x[:1]),) * 2
    return x[-1:], x[:1]


def row_neighbours(last, first):
    cuts = lax.axis_size("cuts")
    if cuts == 1:
        return first, last
    up = [(i, (i + 1) % cuts) for i in range(cuts)]
    before = lax.ppermute(last, "cuts", up)
    if cuts == 2:
        return before, before
    return before, lax.ppermute(first, "cuts", [(j, i) for i, j in up])


def lag_distances(tm):
    return [1 << i for i in range(max(tm - 1, 1).bit_length())]


def cycle_of(sums, first_lag, scales):
    rows, cols = sums.shape
    wide = (rows, cols)
    distances = lag_distances(lax.axis_size("tm"))
    n = len(distances)
    older, window, got = None, sums, first_lag
    for i, d in enumerate(distances):
        if i > 0:
            got = along_tm(window, d)
        if i == n - 1:
            break

        def extend(c, got, window, older=None, i=i, d=d):
            got = jnp.where(lax.axis_index("tm") >= d, got, 0.0)
            further = got if older is None else older + c[:, i : i + 1] * got
            return further, window + c[:, n + i : n + i + 1] * got

        extra = () if older is None else (older,)
        older, window = tiny(extend, [wide] * 2, scales, got, window, *extra)

    def estimate_of(c, got, whole, older=None):
        got = jnp.where(lax.axis_index("tm") >= distances[-1], got, 0.0)
        total = got if older is None else older + c[:, n - 1 : n] * got
        total = whole + c[:, 2 * n : 2 * n + 1] * total + total
        x = total * c[:, 2 * n + 1 : 2 * n + 2]
        return x, *row_edges(x)

    extra = () if older is None else (older,)
    edge = (1, cols)
    estimate, last, first = tiny(estimate_of, [wide, edge, edge], scales, got, sums, *extra)
    before, after = row_neighbours(last, first)
    return pl.pallas_call(
        smooth_kernel,
        out_shape=jax.ShapeDtypeStruct((8, cols), F32),
        in_specs=[VMEM] * 3,
        out_specs=VMEM,
        name="smooth",
        **params(1 << 16, 1 << 16),
    )(estimate, before, after)


def local(turns, shifts, bands, memory):
    half, rows, cols = turns.shape
    angles, count = 2 * half, half * rows
    width = lax.axis_size("col") * cols
    waves = WAVES * rows
    table, turned = (jnp.asarray(t) for t in wave_tables(half, rows))
    core = lax.axis_index("col").astype(jnp.int32)
    distances = lag_distances(lax.axis_size("tm"))
    n = len(PIECES)

    shapes = [jax.ShapeDtypeStruct((count, hi - lo), BF16) for lo, hi in PIECES]
    turns = pltpu.with_memory_space_constraint(turns, pltpu.HBM)
    head = pl.pallas_call(
        head_kernel,
        out_shape=shapes[0],
        in_specs=[ANY],
        out_specs=VMEM,
        scratch_shapes=[
            pltpu.VMEM((half, rows, PIECES[0][1]), BF16),
            pltpu.SemaphoreType.DMA((4,)),
        ],
        name="head",
        **params(count * cols, count * cols),
    )(turns)
    *pieces, sums = pl.pallas_call(
        split_kernel,
        out_shape=(*shapes[1:], jax.ShapeDtypeStruct((rows, cols), F32)),
        in_specs=[ANY],
        out_specs=[VMEM] * n,
        scratch_shapes=[pltpu.VMEM(turns.shape, BF16), pltpu.SemaphoreType.DMA((4,))],
        name="split",
        **params(16 * count * cols, 4 * count * cols),
    )(turns)
    pieces = [head, *pieces]
    spec, gain, scales = pl.pallas_call(
        functools.partial(spec_kernel, rows, distances, angles),
        out_shape=(
            jax.ShapeDtypeStruct((waves, cols), F32),
            jax.ShapeDtypeStruct((waves, 1), F32),
            jax.ShapeDtypeStruct((rows, 128), F32),
        ),
        in_specs=[SMEM] * 2 + [VMEM] * (1 + n),
        out_specs=[VMEM] * 3,
        name="spec",
        **params(2 * waves * count * cols, 4 * count * cols),
    )(bands, memory, table, *pieces)
    first_lag = along_tm(sums, 1)
    cycle = cycle_of(sums, first_lag, scales)
    olds = []
    for i, x in enumerate(pieces):
        olds.append(along_tm(x, 1, wrap=i in WRAPS))
    offset = (shifts + core.reshape(1) * cols) % width
    taps = pl.pallas_call(
        tap_kernel,
        out_shape=jax.ShapeDtypeStruct((TAP_ROWS, 2 * width), BF16),
        in_specs=[SMEM],
        out_specs=VMEM,
        name="taps",
        **params(1 << 20, 1 << 20),
    )(offset)

    def damp(i):
        stage = STAGES[i]
        lo, hi = PIECES[stage[0]][0], PIECES[stage[-1]][1]
        shape = jax.ShapeDtypeStruct((count, hi - lo), BF16)
        inputs = [olds[j] for j in stage] + [pieces[j] for j in stage]
        inputs += [spec, gain, table, turned, cycle]
        spare = (count, hi - lo) if len(stage) > 1 else (16, 128)
        keep, send = pl.pallas_call(
            functools.partial(damp_kernel, lo, rows, len(stage)),
            out_shape=(shape, shape),
            in_specs=[VMEM] * len(inputs),
            out_specs=[VMEM] * 2,
            scratch_shapes=[pltpu.VMEM((count, hi - lo), BF16), pltpu.VMEM(spare, BF16)],
            **params(6 * waves * count * (hi - lo), 8 * count * (hi - lo)),
        )(*inputs)
        recv = lax.ppermute(send, "col", [(0, 1), (1, 0)])
        return (lo, cols + lo), (keep, recv)

    def accumulate(part, acc, last):
        starts, data = part
        inputs = [*data, taps] + ([] if acc is None else [acc])
        kernel = functools.partial(filter_kernel, starts, acc is None, last, rows)
        depth = sum(x.shape[1] for x in data)
        cost = params(2 * count * depth * width, 8 * count * width)
        specs = [VMEM] * len(inputs)
        if last:
            return pl.pallas_call(
                kernel,
                grid=(count // 256,),
                out_shape=jax.ShapeDtypeStruct((half, rows, width), BF16),
                in_specs=specs,
                out_specs=pl.BlockSpec((256 // rows, rows, width), lambda g: (g, 0, 0)),
                name="finish",
                **cost,
            )(*inputs)
        return pl.pallas_call(
            kernel,
            out_shape=jax.ShapeDtypeStruct((count, width), F32),
            in_specs=specs,
            out_specs=VMEM,
            input_output_aliases={} if acc is None else {len(inputs) - 1: 0},
            **cost,
        )(*inputs)

    acc = None
    for i in range(len(STAGES)):
        acc = accumulate(damp(i), acc, i == len(STAGES) - 1)
    return acc


def solution(mesh):
    placed = (
        P(("groups", "tm"), "cuts", "col"),
        P(("groups", "tm")),
        P(("groups", "cuts")),
        P(("groups", "cuts")),
    )

    return jax.shard_map(
        local,
        mesh=mesh,
        in_specs=placed,
        out_specs=P(("groups", "tm", "col"), "cuts", None),
        check_vma=False,
    )
```

```python
import functools
import math

import jax
import jax.numpy as jnp
import numpy as np
from jax import lax
from jax.experimental import pallas as pl
from jax.experimental.pallas import tpu as pltpu
from jax.sharding import PartitionSpec as P

BAND_FREQS = 64
WAVES = 2 * BAND_FREQS
TAP_ROWS = 256
FINISH = 2
PIECES = ((0, 128), (128, 256), (256, 512), (512, 640))
STAGES = ((0, 1), (2,), (3,))
WRAPS = (0, 1)

VMEM = pl.BlockSpec(memory_space=pltpu.VMEM)
SMEM = pl.BlockSpec(memory_space=pltpu.SMEM)
ANY = pl.BlockSpec(memory_space=pl.ANY)
F32 = jnp.float32
BF16 = jnp.bfloat16


def wave_tables(half, rows):
    k = np.arange(BAND_FREQS)[:, None] + 1
    m = (k * np.arange(half)[None, :]) % (2 * half)
    phase = m.astype(np.float64) * (2.0 * math.pi / (2 * half))
    waves = np.concatenate([np.cos(phase), np.sin(phase)], axis=0).astype(np.float32)
    eye = np.eye(rows, dtype=np.float32)
    spread = (waves[:, None, :, None] * eye[None, :, None, :]).reshape(WAVES * rows, half * rows)
    return spread.astype(jnp.bfloat16), np.ascontiguousarray(spread.T).astype(jnp.bfloat16)


def params(flops, size, grant=8 << 20):
    return dict(
        compiler_params=pltpu.CompilerParams(vmem_limit_bytes=grant),
        cost_estimate=pl.CostEstimate(flops=flops, bytes_accessed=size, transcendentals=0),
    )


def pattern(shape, dim, rows):
    return lax.broadcasted_iota(jnp.int32, shape, dim) % rows


def fetch(raw, buffer, sems, columns):
    count = sems.shape[0]
    block = raw.shape[0] // count
    parts = [pl.ds(i * block, block) for i in range(count)]
    copies = [
        pltpu.make_async_copy(raw.at[p, :, columns], buffer.at[p], sems.at[i])
        for i, p in enumerate(parts)
    ]
    for copy in copies:
        copy.start()
    return copies


def head_kernel(raw, out, buffer, sems):
    half, rows, cols = buffer.shape
    block = half // sems.shape[0]
    for i, copy in enumerate(fetch(raw, buffer, sems, pl.ds(*PIECES[0]))):
        copy.wait()
        x = buffer[i * block : (i + 1) * block].reshape(block * rows, cols)
        out[i * block * rows : (i + 1) * block * rows, :] = x


def split_kernel(raw, *refs):
    *pieces, sums, buffer, sems = refs
    half, rows, cols = buffer.shape
    block = half // sems.shape[0]
    shape = (8, block * rows)
    pick = pattern(shape, 1, rows) == lax.broadcasted_iota(jnp.int32, shape, 0)
    pick = pick.astype(F32).astype(BF16)
    total = None
    for i, copy in enumerate(fetch(raw, buffer, sems, pl.ds(0, cols))):
        copy.wait()
        x = buffer[i * block : (i + 1) * block].reshape(block * rows, cols)
        for (lo, hi), out in zip(PIECES[1:], pieces):
            out[i * block * rows : (i + 1) * block * rows, :] = x[:, lo:hi]
        part = jnp.dot(pick, x, preferred_element_type=F32)
        total = part if total is None else total + part
    sums[...] = total[:rows, :]


def spec_kernel(rows, distances, angles, bands, memory, table, *refs):
    *pieces, spec, gain, scales = refs
    waves = spec.shape[0]
    index = lax.broadcasted_iota(jnp.int32, (waves, 1), 0)
    k = index // rows % BAND_FREQS + 1
    flip = jnp.where(k % 2 == 0, 1.0, -1.0)
    for (lo, hi), piece in zip(PIECES, pieces):
        spec[:, lo:hi] = flip * jnp.dot(table[...], piece[...], preferred_element_type=F32)
    band = jnp.full((waves, 1), bands[0], jnp.int32)
    row = lax.broadcasted_iota(jnp.int32, (rows, 1), 0)
    decay = jnp.full((rows, 1), memory[0], F32)
    for s in range(1, rows):
        band = jnp.where(index % rows == s, bands[s], band)
        decay = jnp.where(row == s, memory[s], decay)
    square = (k * k).astype(F32)
    gain[...] = jnp.exp(-square / (2.0 * (band * band).astype(F32))) * (2.0 / angles)
    power, done = decay, 1
    for i, d in enumerate(distances):
        while done < d:
            power, done = power * power, 2 * done
        scales[:, i : i + 1] = jnp.ones_like(decay) if d == 1 else power / decay
        scales[:, len(distances) + i : len(distances) + i + 1] = power
    weight = jnp.ones_like(decay)
    steps = lax.axis_index("tm")
    for j in range(lax.axis_size("tm") - 1):
        weight = jnp.where(j < steps, weight * decay + 1.0, weight)
    scales[:, 2 * len(distances) : 2 * len(distances) + 1] = decay
    scales[:, 2 * len(distances) + 1 : 2 * len(distances) + 2] = 1.0 / (weight * angles)


def smooth_kernel(estimate, before, after, out):
    rows, cols = estimate.shape
    x = estimate[...]
    place = lax.axis_index("cuts")
    first = jnp.where(place != 0, before[...], 0.0)
    last = jnp.where(place != lax.axis_size("cuts") - 1, after[...], 0.0)
    up = jnp.concatenate([first, x[:-1]], axis=0)
    down = jnp.concatenate([x[1:], last], axis=0)
    ring = (up + 2.0 * x + down) * 0.25
    row = pattern((8, cols), 0, rows)
    total = jnp.broadcast_to(ring[:1], (8, cols))
    for s in range(1, rows):
        total = jnp.where(row == s, jnp.broadcast_to(ring[s : s + 1], (8, cols)), total)
    out[...] = total


def damp_kernel(lo, rows, parts, *refs):
    pieces, owns = refs[:parts], refs[parts : 2 * parts]
    spec, gain, table, turned, cycle, keep, send, old, own = refs[2 * parts :]
    count, cols = old.shape
    waves = turned.shape[1]
    core = lax.axis_index("col")
    at = 0
    for piece, mine in zip(pieces, owns):
        place = slice(at, at + piece.shape[1])
        at = place.stop
        older = piece[...]
        old[:, place] = jnp.where(lax.axis_index("tm") > 0, older, jnp.zeros_like(older))
        if parts > 1:
            own[:, place] = mine[...]
    if parts == 1:
        own = owns[0]
    total = jnp.dot(table[...], old[...], preferred_element_type=F32)
    total = (total + spec[:, lo : lo + cols]) * gain[...]
    index = lax.broadcasted_iota(jnp.int32, (waves, 1), 0)
    k = index // rows % BAND_FREQS + 1
    flip = jnp.where(k % 2 == 0, 1.0, -1.0)
    ring = cycle[:, lo : lo + cols]

    def damp(half, source, target):
        scaled = (total if half == 0 else total * flip).astype(BF16)
        for r in range(0, count, 256):
            low = jnp.dot(turned[r : r + 256, :], scaled, preferred_element_type=F32)
            rest = source[r : r + 256, :].astype(F32) - low
            rest = rest.reshape(32, 8, cols) - ring[None]
            target[r : r + 256, :] = rest.reshape(256, cols).astype(BF16)

    @pl.when(core == 0)
    def _():
        damp(1, own, send)
        damp(0, old, keep)

    @pl.when(core != 0)
    def _():
        damp(0, old, send)
        damp(1, own, keep)


def filter_kernel(starts, first, last, rows, *refs):
    n = len(starts)
    taps = refs[n]
    acc = None if first else refs[n + 1]
    out = refs[-1]
    width = out.shape[-1]
    count = refs[0].shape[0]
    step = count // FINISH if last else 256

    depth = refs[0].shape[1]
    offs = [(-start) % width for start in starts]
    if n * depth <= TAP_ROWS:
        weights = [jnp.concatenate([taps[:depth, o : o + width] for o in offs], axis=0)]
    else:
        weights = [taps[:depth, o : o + width] for o in offs]

    def block(r):
        total = None if first else acc[r, :]
        data = [ref[r, :] for ref in refs[:n]]
        if len(weights) == 1:
            data = [jnp.concatenate(data, axis=1)]
        for x, w in zip(data, weights):
            part = jnp.dot(x, w, preferred_element_type=F32)
            total = part if total is None else total + part
        return total

    if last:
        r = pl.ds(pl.multiple_of(pl.program_id(0) * step, step), step)
        out[...] = block(r).astype(BF16).reshape(step // rows, rows, width)
    else:
        for b in range(0, count, step):
            out[b : b + step, :] = block(slice(b, b + step))


def tap_kernel(shift, out):
    width = out.shape[1] // 2
    lanes = 128
    for r in range(0, lanes, 16):
        row = lax.broadcasted_iota(jnp.int32, (16, width), 0) + r
        col = lax.broadcasted_iota(jnp.int32, (16, width), 1)
        lag = col - row - shift[0]
        lag = jnp.where(lag < 0, lag + width, lag)
        lag = jnp.where(lag < 0, lag + width, lag)
        near = jnp.minimum(lag, width - lag)
        size = jnp.maximum(near, 1).astype(F32)
        odd = -1.0 / (math.pi**2 * size**2)
        tap = jnp.where(near == 0, 0.25, jnp.where((near & 1) == 1, odd, 0.0)).astype(BF16)
        for b in range(out.shape[0] // lanes):
            for c in range(0, 2 * width, width):
                start = (c + b * lanes) % (2 * width)
                rows = slice(b * lanes + r, b * lanes + r + 16)
                room = min(width, 2 * width - start)
                out[rows, start : start + room] = tap[:, :room]
                if room < width:
                    out[rows, : width - room] = tap[:, room:]


def along_tm(x, distance, wrap=True):
    tm = lax.axis_size("tm")
    route = [(i, (i + distance) % tm) for i in range(tm if wrap else tm - distance)]
    return lax.ppermute(x, "tm", route)


def tiny(body, shapes, *args):
    def kernel(*refs):
        for ref, value in zip(refs[len(args) :], body(*(r[...] for r in refs[: len(args)]))):
            ref[...] = value

    return pl.pallas_call(
        kernel,
        out_shape=tuple(jax.ShapeDtypeStruct(s, F32) for s in shapes),
        in_specs=[VMEM] * len(args),
        out_specs=(VMEM,) * len(shapes),
        **params(1 << 16, 1 << 16),
    )(*args)


def row_edges(x):
    place = lax.axis_index("cuts")
    if lax.axis_size("cuts") == 2:
        return (jnp.where(place == 0, x[-1:], x[:1]),)
    return x[-1:], x[:1]


def row_neighbours(last, first=None):
    cuts = lax.axis_size("cuts")
    if cuts == 1:
        return last, last
    up = [(i, (i + 1) % cuts) for i in range(cuts)]
    before = lax.ppermute(last, "cuts", up)
    if cuts == 2:
        return before, before
    return before, lax.ppermute(first, "cuts", [(j, i) for i, j in up])


def lag_distances(tm):
    return [1 << i for i in range(max(tm - 1, 1).bit_length())]


def cycle_of(sums, first_lag, scales):
    rows, cols = sums.shape
    wide = (rows, cols)
    distances = lag_distances(lax.axis_size("tm"))
    n = len(distances)
    older, window, got = None, sums, first_lag
    for i, d in enumerate(distances):
        if i > 0:
            got = along_tm(window, d)
        if i == n - 1:
            break

        def extend(c, got, window, older=None, i=i, d=d):
            got = jnp.where(lax.axis_index("tm") >= d, got, 0.0)
            further = got if older is None else older + c[:, i : i + 1] * got
            return further, window + c[:, n + i : n + i + 1] * got

        extra = () if older is None else (older,)
        older, window = tiny(extend, [wide] * 2, scales, got, window, *extra)

    def estimate_of(c, got, whole, older=None):
        got = jnp.where(lax.axis_index("tm") >= distances[-1], got, 0.0)
        total = got if older is None else older + c[:, n - 1 : n] * got
        total = whole + c[:, 2 * n : 2 * n + 1] * total + total
        x = total * c[:, 2 * n + 1 : 2 * n + 2]
        return x, *row_edges(x)

    extra = () if older is None else (older,)
    edge = (1, cols)
    edges = [edge] * (1 if lax.axis_size("cuts") == 2 else 2)
    estimate, *ends = tiny(estimate_of, [wide, *edges], scales, got, sums, *extra)
    before, after = row_neighbours(*ends)
    return pl.pallas_call(
        smooth_kernel,
        out_shape=jax.ShapeDtypeStruct((8, cols), F32),
        in_specs=[VMEM] * 3,
        out_specs=VMEM,
        name="smooth",
        **params(1 << 16, 1 << 16),
    )(estimate, before, after)


def local(turns, shifts, bands, memory):
    half, rows, cols = turns.shape
    angles, count = 2 * half, half * rows
    width = lax.axis_size("col") * cols
    waves = WAVES * rows
    table, turned = (jnp.asarray(t) for t in wave_tables(half, rows))
    core = lax.axis_index("col").astype(jnp.int32)
    distances = lag_distances(lax.axis_size("tm"))
    n = len(PIECES)

    shapes = [jax.ShapeDtypeStruct((count, hi - lo), BF16) for lo, hi in PIECES]
    turns = pltpu.with_memory_space_constraint(turns, pltpu.HBM)
    head = pl.pallas_call(
        head_kernel,
        out_shape=shapes[0],
        in_specs=[ANY],
        out_specs=VMEM,
        scratch_shapes=[
            pltpu.VMEM((half, rows, PIECES[0][1]), BF16),
            pltpu.SemaphoreType.DMA((4,)),
        ],
        name="head",
        **params(count * cols, count * cols),
    )(turns)
    *pieces, sums = pl.pallas_call(
        split_kernel,
        out_shape=(*shapes[1:], jax.ShapeDtypeStruct((rows, cols), F32)),
        in_specs=[ANY],
        out_specs=[VMEM] * n,
        scratch_shapes=[pltpu.VMEM(turns.shape, BF16), pltpu.SemaphoreType.DMA((4,))],
        name="split",
        **params(16 * count * cols, 4 * count * cols),
    )(turns)
    pieces = [head, *pieces]
    spec, gain, scales = pl.pallas_call(
        functools.partial(spec_kernel, rows, distances, angles),
        out_shape=(
            jax.ShapeDtypeStruct((waves, cols), F32),
            jax.ShapeDtypeStruct((waves, 1), F32),
            jax.ShapeDtypeStruct((rows, 128), F32),
        ),
        in_specs=[SMEM] * 2 + [VMEM] * (1 + n),
        out_specs=[VMEM] * 3,
        name="spec",
        **params(2 * waves * count * cols, 4 * count * cols),
    )(bands, memory, table, *pieces)
    first_lag = along_tm(sums, 1)
    cycle = cycle_of(sums, first_lag, scales)
    olds = []
    for i, x in enumerate(pieces):
        olds.append(along_tm(x, 1, wrap=i in WRAPS))
    offset = (shifts + core.reshape(1) * cols) % width
    taps = pl.pallas_call(
        tap_kernel,
        out_shape=jax.ShapeDtypeStruct((TAP_ROWS, 2 * width), BF16),
        in_specs=[SMEM],
        out_specs=VMEM,
        name="taps",
        **params(1 << 20, 1 << 20),
    )(offset)

    def damp(i):
        stage = STAGES[i]
        lo, hi = PIECES[stage[0]][0], PIECES[stage[-1]][1]
        shape = jax.ShapeDtypeStruct((count, hi - lo), BF16)
        inputs = [olds[j] for j in stage] + [pieces[j] for j in stage]
        inputs += [spec, gain, table, turned, cycle]
        spare = (count, hi - lo) if len(stage) > 1 else (16, 128)
        keep, send = pl.pallas_call(
            functools.partial(damp_kernel, lo, rows, len(stage)),
            out_shape=(shape, shape),
            in_specs=[VMEM] * len(inputs),
            out_specs=[VMEM] * 2,
            scratch_shapes=[pltpu.VMEM((count, hi - lo), BF16), pltpu.VMEM(spare, BF16)],
            **params(6 * waves * count * (hi - lo), 8 * count * (hi - lo)),
        )(*inputs)
        recv = lax.ppermute(send, "col", [(0, 1), (1, 0)])
        return (lo, cols + lo), (keep, recv)

    def accumulate(part, acc, last):
        starts, data = part
        inputs = [*data, taps] + ([] if acc is None else [acc])
        kernel = functools.partial(filter_kernel, starts, acc is None, last, rows)
        depth = sum(x.shape[1] for x in data)
        cost = params(2 * count * depth * width, 8 * count * width)
        specs = [VMEM] * len(inputs)
        if last:
            return pl.pallas_call(
                kernel,
                grid=(FINISH,),
                out_shape=jax.ShapeDtypeStruct((half, rows, width), BF16),
                in_specs=specs,
                out_specs=pl.BlockSpec((half // FINISH, rows, width), lambda g: (g, 0, 0)),
                name="finish",
                **cost,
            )(*inputs)
        return pl.pallas_call(
            kernel,
            out_shape=jax.ShapeDtypeStruct((count, width), F32),
            in_specs=specs,
            out_specs=VMEM,
            input_output_aliases={} if acc is None else {len(inputs) - 1: 0},
            **cost,
        )(*inputs)

    acc = None
    for i in range(len(STAGES)):
        acc = accumulate(damp(i), acc, i == len(STAGES) - 1)
    return acc


def solution(mesh):
    placed = (
        P(("groups", "tm"), "cuts", "col"),
        P(("groups", "tm")),
        P(("groups", "cuts")),
        P(("groups", "cuts")),
    )

    return jax.shard_map(
        local,
        mesh=mesh,
        in_specs=placed,
        out_specs=P(("groups", "tm", "col"), "cuts", None),
        check_vma=False,
    )
```

```python
import functools
import math

import jax
import jax.numpy as jnp
import numpy as np
from jax import lax
from jax.experimental import pallas as pl
from jax.experimental.pallas import tpu as pltpu
from jax.sharding import PartitionSpec as P

BAND_FREQS = 64
WAVES = 2 * BAND_FREQS
TAP_ROWS = 256
FINISH = 2
PIECES = ((0, 128), (128, 256), (256, 512), (512, 640))
STAGES = ((0, 1), (2,), (3,))
WRAPS = (0, 1)

VMEM = pl.BlockSpec(memory_space=pltpu.VMEM)
SMEM = pl.BlockSpec(memory_space=pltpu.SMEM)
ANY = pl.BlockSpec(memory_space=pl.ANY)
F32 = jnp.float32
BF16 = jnp.bfloat16


def wave_tables(half, rows):
    k = np.arange(BAND_FREQS)[:, None] + 1
    m = (k * np.arange(half)[None, :]) % (2 * half)
    phase = m.astype(np.float64) * (2.0 * math.pi / (2 * half))
    waves = np.concatenate([np.cos(phase), np.sin(phase)], axis=0).astype(np.float32)
    eye = np.eye(rows, dtype=np.float32)
    spread = (waves[:, None, :, None] * eye[None, :, None, :]).reshape(WAVES * rows, half * rows)
    return spread.astype(jnp.bfloat16), np.ascontiguousarray(spread.T).astype(jnp.bfloat16)


def params(flops, size, grant=8 << 20):
    return dict(
        compiler_params=pltpu.CompilerParams(vmem_limit_bytes=grant),
        cost_estimate=pl.CostEstimate(flops=flops, bytes_accessed=size, transcendentals=0),
    )


def pattern(shape, dim, rows):
    return lax.broadcasted_iota(jnp.int32, shape, dim) % rows


def fetch(raw, buffer, sems, columns):
    count = sems.shape[0]
    block = raw.shape[0] // count
    parts = [pl.ds(i * block, block) for i in range(count)]
    copies = [
        pltpu.make_async_copy(raw.at[p, :, columns], buffer.at[p], sems.at[i])
        for i, p in enumerate(parts)
    ]
    for copy in copies:
        copy.start()
    return copies


def head_kernel(raw, out, buffer, sems):
    half, rows, cols = buffer.shape
    block = half // sems.shape[0]
    for i, copy in enumerate(fetch(raw, buffer, sems, pl.ds(*PIECES[0]))):
        copy.wait()
        x = buffer[i * block : (i + 1) * block].reshape(block * rows, cols)
        out[i * block * rows : (i + 1) * block * rows, :] = x


def split_kernel(raw, *refs):
    *pieces, sums, buffer, sems = refs
    half, rows, cols = buffer.shape
    block = half // sems.shape[0]
    shape = (8, block * rows)
    pick = pattern(shape, 1, rows) == lax.broadcasted_iota(jnp.int32, shape, 0)
    pick = pick.astype(F32).astype(BF16)
    total = None
    for i, copy in enumerate(fetch(raw, buffer, sems, pl.ds(0, cols))):
        copy.wait()
        x = buffer[i * block : (i + 1) * block].reshape(block * rows, cols)
        for (lo, hi), out in zip(PIECES[1:], pieces):
            out[i * block * rows : (i + 1) * block * rows, :] = x[:, lo:hi]
        part = jnp.dot(pick, x, preferred_element_type=F32)
        total = part if total is None else total + part
    sums[...] = total[:rows, :]


def spec_kernel(rows, distances, angles, bands, memory, table, *refs):
    *pieces, spec, gain, scales, local_table, local_bands, local_memory, sems = refs
    pairs = [(bands, local_bands), (memory, local_memory), (table, local_table)]
    copies = [pltpu.make_async_copy(a, b, sems.at[i]) for i, (a, b) in enumerate(pairs)]
    for copy in copies:
        copy.start()
    for copy in copies:
        copy.wait()
    bands, memory, table = local_bands, local_memory, local_table
    waves = spec.shape[0]
    index = lax.broadcasted_iota(jnp.int32, (waves, 1), 0)
    k = index // rows % BAND_FREQS + 1
    flip = jnp.where(k % 2 == 0, 1.0, -1.0)
    for (lo, hi), piece in zip(PIECES, pieces):
        spec[:, lo:hi] = flip * jnp.dot(table[...], piece[...], preferred_element_type=F32)
    band = jnp.full((waves, 1), bands[0], jnp.int32)
    row = lax.broadcasted_iota(jnp.int32, (rows, 1), 0)
    decay = jnp.full((rows, 1), memory[0], F32)
    for s in range(1, rows):
        band = jnp.where(index % rows == s, bands[s], band)
        decay = jnp.where(row == s, memory[s], decay)
    square = (k * k).astype(F32)
    gain[...] = jnp.exp(-square / (2.0 * (band * band).astype(F32))) * (2.0 / angles)
    power, done = decay, 1
    for i, d in enumerate(distances):
        while done < d:
            power, done = power * power, 2 * done
        scales[:, i : i + 1] = jnp.ones_like(decay) if d == 1 else power / decay
        scales[:, len(distances) + i : len(distances) + i + 1] = power
    weight = jnp.ones_like(decay)
    steps = lax.axis_index("tm")
    for j in range(lax.axis_size("tm") - 1):
        weight = jnp.where(j < steps, weight * decay + 1.0, weight)
    scales[:, 2 * len(distances) : 2 * len(distances) + 1] = decay
    scales[:, 2 * len(distances) + 1 : 2 * len(distances) + 2] = 1.0 / (weight * angles)


def smooth_kernel(estimate, before, after, out):
    rows, cols = estimate.shape
    x = estimate[...]
    place = lax.axis_index("cuts")
    first = jnp.where(place != 0, before[...], 0.0)
    last = jnp.where(place != lax.axis_size("cuts") - 1, after[...], 0.0)
    up = jnp.concatenate([first, x[:-1]], axis=0)
    down = jnp.concatenate([x[1:], last], axis=0)
    ring = (up + 2.0 * x + down) * 0.25
    row = pattern((8, cols), 0, rows)
    total = jnp.broadcast_to(ring[:1], (8, cols))
    for s in range(1, rows):
        total = jnp.where(row == s, jnp.broadcast_to(ring[s : s + 1], (8, cols)), total)
    out[...] = total


def damp_kernel(lo, rows, parts, late, *refs):
    pieces, owns = refs[:parts], refs[parts : 2 * parts]
    spec, gain, table, turned, cycle, keep, send, old, own = refs[2 * parts :]
    count, cols = old.shape
    waves = turned.shape[1]
    core = lax.axis_index("col")
    at = 0
    for piece, mine in zip(pieces, owns):
        place = slice(at, at + piece.shape[1])
        at = place.stop
        older = piece[...]
        old[:, place] = jnp.where(lax.axis_index("tm") > 0, older, jnp.zeros_like(older))
        if parts > 1:
            own[:, place] = mine[...]
    if parts == 1:
        own = owns[0]
    total = jnp.dot(table[...], old[...], preferred_element_type=F32)
    total = (total + spec[:, lo : lo + cols]) * gain[...]
    index = lax.broadcasted_iota(jnp.int32, (waves, 1), 0)
    k = index // rows % BAND_FREQS + 1
    flip = jnp.where(k % 2 == 0, 1.0, -1.0)
    ring = cycle[:, lo : lo + cols]

    def damp(half, source, target):
        scaled = (total if half == 0 else total * flip).astype(BF16)
        for r in range(0, count, 256):
            low = jnp.dot(turned[r : r + 256, :], scaled, preferred_element_type=F32)
            rest = source[r : r + 256, :].astype(F32) - low
            rest = rest.reshape(32, 8, cols) - ring[None]
            target[r : r + 256, :] = rest.reshape(256, cols).astype(BF16)

    def both(sent, kept, source, held):
        damp(sent, source, send)
        if late:
            keep[...] = (total if kept == 0 else total * flip).astype(BF16)
        else:
            damp(kept, held, keep)

    @pl.when(core == 0)
    def _():
        both(1, 0, own, old)

    @pl.when(core != 0)
    def _():
        both(0, 1, old, own)


def hold_kernel(lo, piece, own, scaled, turned, cycle, keep):
    count, cols = own.shape
    ring = cycle[:, lo : lo + cols]

    def damp(source):
        for r in range(0, count, 256):
            low = jnp.dot(turned[r : r + 256, :], scaled[...], preferred_element_type=F32)
            rest = source(slice(r, r + 256)).astype(F32) - low
            rest = rest.reshape(32, 8, cols) - ring[None]
            keep[r : r + 256, :] = rest.reshape(256, cols).astype(BF16)

    @pl.when(lax.axis_index("col") == 0)
    def _():
        here = lax.axis_index("tm") > 0
        damp(lambda r: jnp.where(here, piece[r, :], jnp.zeros((256, cols), BF16)))

    @pl.when(lax.axis_index("col") != 0)
    def _():
        damp(lambda r: own[r, :])


def filter_kernel(starts, first, last, rows, *refs):
    n = len(starts)
    taps = refs[n]
    acc = None if first else refs[n + 1]
    out = refs[-1]
    width = out.shape[-1]
    count = refs[0].shape[0]
    step = count // FINISH if last else 256

    depth = refs[0].shape[1]
    offs = [(-start) % width for start in starts]
    if n * depth <= TAP_ROWS:
        weights = [jnp.concatenate([taps[:depth, o : o + width] for o in offs], axis=0)]
    else:
        weights = [taps[:depth, o : o + width] for o in offs]

    def block(r):
        total = None if first else acc[r, :]
        data = [ref[r, :] for ref in refs[:n]]
        if len(weights) == 1:
            data = [jnp.concatenate(data, axis=1)]
        for x, w in zip(data, weights):
            part = jnp.dot(x, w, preferred_element_type=F32)
            total = part if total is None else total + part
        return total

    if last:
        r = pl.ds(pl.multiple_of(pl.program_id(0) * step, step), step)
        out[...] = block(r).astype(BF16).reshape(step // rows, rows, width)
    else:
        for b in range(0, count, step):
            out[b : b + step, :] = block(slice(b, b + step))


def tap_kernel(shift, out):
    width = out.shape[1] // 2
    lanes = 128
    for r in range(0, lanes, 16):
        row = lax.broadcasted_iota(jnp.int32, (16, width), 0) + r
        col = lax.broadcasted_iota(jnp.int32, (16, width), 1)
        lag = col - row - shift[0]
        lag = jnp.where(lag < 0, lag + width, lag)
        lag = jnp.where(lag < 0, lag + width, lag)
        near = jnp.minimum(lag, width - lag)
        size = jnp.maximum(near, 1).astype(F32)
        odd = -1.0 / (math.pi**2 * size**2)
        tap = jnp.where(near == 0, 0.25, jnp.where((near & 1) == 1, odd, 0.0)).astype(BF16)
        for b in range(out.shape[0] // lanes):
            for c in range(0, 2 * width, width):
                start = (c + b * lanes) % (2 * width)
                rows = slice(b * lanes + r, b * lanes + r + 16)
                room = min(width, 2 * width - start)
                out[rows, start : start + room] = tap[:, :room]
                if room < width:
                    out[rows, : width - room] = tap[:, room:]


def along_tm(x, distance, wrap=True):
    tm = lax.axis_size("tm")
    route = [(i, (i + distance) % tm) for i in range(tm if wrap else tm - distance)]
    return lax.ppermute(x, "tm", route)


def tiny(body, shapes, *args):
    def kernel(*refs):
        for ref, value in zip(refs[len(args) :], body(*(r[...] for r in refs[: len(args)]))):
            ref[...] = value

    return pl.pallas_call(
        kernel,
        out_shape=tuple(jax.ShapeDtypeStruct(s, F32) for s in shapes),
        in_specs=[VMEM] * len(args),
        out_specs=(VMEM,) * len(shapes),
        **params(1 << 16, 1 << 16),
    )(*args)


def row_edges(x):
    place = lax.axis_index("cuts")
    if lax.axis_size("cuts") == 2:
        return (jnp.where(place == 0, x[-1:], x[:1]),)
    return x[-1:], x[:1]


def row_neighbours(last, first=None):
    cuts = lax.axis_size("cuts")
    if cuts == 1:
        return last, last
    up = [(i, (i + 1) % cuts) for i in range(cuts)]
    before = lax.ppermute(last, "cuts", up)
    if cuts == 2:
        return before, before
    return before, lax.ppermute(first, "cuts", [(j, i) for i, j in up])


def lag_distances(tm):
    return [1 << i for i in range(max(tm - 1, 1).bit_length())]


def cycle_of(sums, first_lag, scales):
    rows, cols = sums.shape
    wide = (rows, cols)
    distances = lag_distances(lax.axis_size("tm"))
    n = len(distances)
    older, window, got = None, sums, first_lag
    for i, d in enumerate(distances):
        if i > 0:
            got = along_tm(window, d)
        if i == n - 1:
            break

        def extend(c, got, window, older=None, i=i, d=d):
            got = jnp.where(lax.axis_index("tm") >= d, got, 0.0)
            further = got if older is None else older + c[:, i : i + 1] * got
            return further, window + c[:, n + i : n + i + 1] * got

        extra = () if older is None else (older,)
        older, window = tiny(extend, [wide] * 2, scales, got, window, *extra)

    def estimate_of(c, got, whole, older=None):
        got = jnp.where(lax.axis_index("tm") >= distances[-1], got, 0.0)
        total = got if older is None else older + c[:, n - 1 : n] * got
        total = whole + c[:, 2 * n : 2 * n + 1] * total + total
        x = total * c[:, 2 * n + 1 : 2 * n + 2]
        return x, *row_edges(x)

    extra = () if older is None else (older,)
    edge = (1, cols)
    edges = [edge] * (1 if lax.axis_size("cuts") == 2 else 2)
    estimate, *ends = tiny(estimate_of, [wide, *edges], scales, got, sums, *extra)
    before, after = row_neighbours(*ends)
    return pl.pallas_call(
        smooth_kernel,
        out_shape=jax.ShapeDtypeStruct((8, cols), F32),
        in_specs=[VMEM] * 3,
        out_specs=VMEM,
        name="smooth",
        **params(1 << 16, 1 << 16),
    )(estimate, before, after)


def local(turns, shifts, bands, memory):
    half, rows, cols = turns.shape
    angles, count = 2 * half, half * rows
    width = lax.axis_size("col") * cols
    waves = WAVES * rows
    table, turned = (jnp.asarray(t) for t in wave_tables(half, rows))
    core = lax.axis_index("col").astype(jnp.int32)
    distances = lag_distances(lax.axis_size("tm"))
    n = len(PIECES)

    shapes = [jax.ShapeDtypeStruct((count, hi - lo), BF16) for lo, hi in PIECES]
    turns = pltpu.with_memory_space_constraint(turns, pltpu.HBM)
    head = pl.pallas_call(
        head_kernel,
        out_shape=shapes[0],
        in_specs=[ANY],
        out_specs=VMEM,
        scratch_shapes=[
            pltpu.VMEM((half, rows, PIECES[0][1]), BF16),
            pltpu.SemaphoreType.DMA((4,)),
        ],
        name="head",
        **params(count * cols, count * cols),
    )(turns)
    *pieces, sums = pl.pallas_call(
        split_kernel,
        out_shape=(*shapes[1:], jax.ShapeDtypeStruct((rows, cols), F32)),
        in_specs=[ANY],
        out_specs=[VMEM] * n,
        scratch_shapes=[pltpu.VMEM(turns.shape, BF16), pltpu.SemaphoreType.DMA((4,))],
        name="split",
        **params(16 * count * cols, 4 * count * cols),
    )(turns)
    pieces = [head, *pieces]
    spec, gain, scales = pl.pallas_call(
        functools.partial(spec_kernel, rows, distances, angles),
        out_shape=(
            jax.ShapeDtypeStruct((waves, cols), F32),
            jax.ShapeDtypeStruct((waves, 1), F32),
            jax.ShapeDtypeStruct((rows, 128), F32),
        ),
        in_specs=[ANY] * 3 + [VMEM] * n,
        out_specs=[VMEM] * 3,
        scratch_shapes=[
            pltpu.VMEM(table.shape, BF16),
            pltpu.SMEM((rows,), jnp.int32),
            pltpu.SMEM((rows,), F32),
            pltpu.SemaphoreType.DMA((3,)),
        ],
        name="spec",
        **params(2 * waves * count * cols, 4 * count * cols),
    )(*(pltpu.with_memory_space_constraint(x, pltpu.HBM) for x in (bands, memory, table)), *pieces)
    first_lag = along_tm(sums, 1)
    cycle = cycle_of(sums, first_lag, scales)
    olds = []
    for i, x in enumerate(pieces):
        olds.append(along_tm(x, 1, wrap=i in WRAPS))
    offset = (shifts + core.reshape(1) * cols) % width
    taps = pl.pallas_call(
        tap_kernel,
        out_shape=jax.ShapeDtypeStruct((TAP_ROWS, 2 * width), BF16),
        in_specs=[SMEM],
        out_specs=VMEM,
        name="taps",
        **params(1 << 20, 1 << 20),
    )(offset)

    def damp(i):
        stage = STAGES[i]
        lo, hi = PIECES[stage[0]][0], PIECES[stage[-1]][1]
        shape = jax.ShapeDtypeStruct((count, hi - lo), BF16)
        inputs = [olds[j] for j in stage] + [pieces[j] for j in stage]
        inputs += [spec, gain, table, turned, cycle]
        spare = (count, hi - lo) if len(stage) > 1 else (16, 128)
        late = i == len(STAGES) - 1
        held = jax.ShapeDtypeStruct((waves, hi - lo), BF16) if late else shape
        keep, send = pl.pallas_call(
            functools.partial(damp_kernel, lo, rows, len(stage), late),
            out_shape=(held, shape),
            in_specs=[VMEM] * len(inputs),
            out_specs=[VMEM] * 2,
            scratch_shapes=[pltpu.VMEM((count, hi - lo), BF16), pltpu.VMEM(spare, BF16)],
            **params(6 * waves * count * (hi - lo), 8 * count * (hi - lo)),
        )(*inputs)
        recv = lax.ppermute(send, "col", [(0, 1), (1, 0)])
        if late:
            (j,) = stage
            keep = pl.pallas_call(
                functools.partial(hold_kernel, lo),
                out_shape=shape,
                in_specs=[VMEM] * 5,
                out_specs=VMEM,
                name="hold",
                **params(2 * waves * count * (hi - lo), 4 * count * (hi - lo)),
            )(olds[j], pieces[j], keep, turned, cycle)
        return (lo, cols + lo), (keep, recv)

    def accumulate(part, acc, last):
        starts, data = part
        inputs = [*data, taps] + ([] if acc is None else [acc])
        kernel = functools.partial(filter_kernel, starts, acc is None, last, rows)
        depth = sum(x.shape[1] for x in data)
        cost = params(2 * count * depth * width, 8 * count * width)
        specs = [VMEM] * len(inputs)
        if last:
            return pl.pallas_call(
                kernel,
                grid=(FINISH,),
                out_shape=jax.ShapeDtypeStruct((half, rows, width), BF16),
                in_specs=specs,
                out_specs=pl.BlockSpec((half // FINISH, rows, width), lambda g: (g, 0, 0)),
                name="finish",
                **cost,
            )(*inputs)
        return pl.pallas_call(
            kernel,
            out_shape=jax.ShapeDtypeStruct((count, width), F32),
            in_specs=specs,
            out_specs=VMEM,
            input_output_aliases={} if acc is None else {len(inputs) - 1: 0},
            **cost,
        )(*inputs)

    acc = None
    for i in range(len(STAGES)):
        starts, data = damp(i)
        if i == len(STAGES) - 2:
            acc = accumulate((starts[:1], data[:1]), acc, False)
            acc = accumulate((starts[1:], data[1:]), acc, False)
        else:
            acc = accumulate((starts, data), acc, i == len(STAGES) - 1)
    return acc


def solution(mesh):
    placed = (
        P(("groups", "tm"), "cuts", "col"),
        P(("groups", "tm")),
        P(("groups", "cuts")),
        P(("groups", "cuts")),
    )

    return jax.shard_map(
        local,
        mesh=mesh,
        in_specs=placed,
        out_specs=P(("groups", "tm", "col"), "cuts", None),
        check_vma=False,
    )
```

```python
import functools
import math

import jax
import jax.numpy as jnp
import numpy as np
from jax import lax
from jax.experimental import pallas as pl
from jax.experimental.pallas import tpu as pltpu
from jax.sharding import PartitionSpec as P

BAND_FREQS = 64
WAVES = 2 * BAND_FREQS
TAP_ROWS = 256
FINISH = 8
PIECES = ((0, 128), (128, 256), (256, 512), (512, 640))
STAGES = ((0, 1), (2,), (3,))
WRAPS = (0, 1)

VMEM = pl.BlockSpec(memory_space=pltpu.VMEM)
SMEM = pl.BlockSpec(memory_space=pltpu.SMEM)
ANY = pl.BlockSpec(memory_space=pl.ANY)
F32 = jnp.float32
BF16 = jnp.bfloat16


def wave_tables(half, rows):
    k = np.arange(BAND_FREQS)[:, None] + 1
    m = (k * np.arange(half)[None, :]) % (2 * half)
    phase = m.astype(np.float64) * (2.0 * math.pi / (2 * half))
    waves = np.concatenate([np.cos(phase), np.sin(phase)], axis=0).astype(np.float32)
    eye = np.eye(rows, dtype=np.float32)
    spread = (waves[:, None, :, None] * eye[None, :, None, :]).reshape(WAVES * rows, half * rows)
    return spread.astype(jnp.bfloat16), np.ascontiguousarray(spread.T).astype(jnp.bfloat16)


def params(flops, size, grant=8 << 20):
    return dict(
        compiler_params=pltpu.CompilerParams(vmem_limit_bytes=grant),
        cost_estimate=pl.CostEstimate(flops=flops, bytes_accessed=size, transcendentals=0),
    )


def pattern(shape, dim, rows):
    return lax.broadcasted_iota(jnp.int32, shape, dim) % rows


def fetch(raw, buffer, sems, columns):
    count = sems.shape[0]
    block = raw.shape[0] // count
    parts = [pl.ds(i * block, block) for i in range(count)]
    copies = [
        pltpu.make_async_copy(raw.at[p, :, columns], buffer.at[p], sems.at[i])
        for i, p in enumerate(parts)
    ]
    for copy in copies:
        copy.start()
    return copies


def head_kernel(raw, out, buffer, sems):
    half, rows, cols = buffer.shape
    block = half // sems.shape[0]
    for i, copy in enumerate(fetch(raw, buffer, sems, pl.ds(*PIECES[0]))):
        copy.wait()
        x = buffer[i * block : (i + 1) * block].reshape(block * rows, cols)
        out[i * block * rows : (i + 1) * block * rows, :] = x


def split_kernel(raw, *refs):
    *pieces, sums, buffer, sems = refs
    half, rows, cols = buffer.shape
    block = half // sems.shape[0]
    shape = (8, block * rows)
    pick = pattern(shape, 1, rows) == lax.broadcasted_iota(jnp.int32, shape, 0)
    pick = pick.astype(F32).astype(BF16)
    total = None
    for i, copy in enumerate(fetch(raw, buffer, sems, pl.ds(0, cols))):
        copy.wait()
        x = buffer[i * block : (i + 1) * block].reshape(block * rows, cols)
        for (lo, hi), out in zip(PIECES[1:], pieces):
            out[i * block * rows : (i + 1) * block * rows, :] = x[:, lo:hi]
        part = jnp.dot(pick, x, preferred_element_type=F32)
        total = part if total is None else total + part
    sums[...] = total[:rows, :]


def spec_kernel(rows, distances, angles, bands, memory, table, *refs):
    *pieces, spec, gain, scales, local_table, local_bands, local_memory, sems = refs
    pairs = [(bands, local_bands), (memory, local_memory), (table, local_table)]
    copies = [pltpu.make_async_copy(a, b, sems.at[i]) for i, (a, b) in enumerate(pairs)]
    for copy in copies:
        copy.start()
    for copy in copies:
        copy.wait()
    bands, memory, table = local_bands, local_memory, local_table
    waves = spec.shape[0]
    index = lax.broadcasted_iota(jnp.int32, (waves, 1), 0)
    k = index // rows % BAND_FREQS + 1
    flip = jnp.where(k % 2 == 0, 1.0, -1.0)
    for (lo, hi), piece in zip(PIECES, pieces):
        spec[:, lo:hi] = flip * jnp.dot(table[...], piece[...], preferred_element_type=F32)
    band = jnp.full((waves, 1), bands[0], jnp.int32)
    row = lax.broadcasted_iota(jnp.int32, (rows, 1), 0)
    decay = jnp.full((rows, 1), memory[0], F32)
    for s in range(1, rows):
        band = jnp.where(index % rows == s, bands[s], band)
        decay = jnp.where(row == s, memory[s], decay)
    square = (k * k).astype(F32)
    gain[...] = jnp.exp(-square / (2.0 * (band * band).astype(F32))) * (2.0 / angles)
    power, done = decay, 1
    for i, d in enumerate(distances):
        while done < d:
            power, done = power * power, 2 * done
        scales[:, i : i + 1] = jnp.ones_like(decay) if d == 1 else power / decay
        scales[:, len(distances) + i : len(distances) + i + 1] = power
    weight = jnp.ones_like(decay)
    steps = lax.axis_index("tm")
    for j in range(lax.axis_size("tm") - 1):
        weight = jnp.where(j < steps, weight * decay + 1.0, weight)
    scales[:, 2 * len(distances) : 2 * len(distances) + 1] = decay
    scales[:, 2 * len(distances) + 1 : 2 * len(distances) + 2] = 1.0 / (weight * angles)


def smooth_kernel(estimate, before, after, out):
    rows, cols = estimate.shape
    x = estimate[...]
    place = lax.axis_index("cuts")
    first = jnp.where(place != 0, before[...], 0.0)
    last = jnp.where(place != lax.axis_size("cuts") - 1, after[...], 0.0)
    up = jnp.concatenate([first, x[:-1]], axis=0)
    down = jnp.concatenate([x[1:], last], axis=0)
    ring = (up + 2.0 * x + down) * 0.25
    row = pattern((8, cols), 0, rows)
    total = jnp.broadcast_to(ring[:1], (8, cols))
    for s in range(1, rows):
        total = jnp.where(row == s, jnp.broadcast_to(ring[s : s + 1], (8, cols)), total)
    out[...] = total


def damp_kernel(lo, rows, parts, late, *refs):
    pieces, owns = refs[:parts], refs[parts : 2 * parts]
    spec, gain, table, turned, cycle, keep, send, old, own = refs[2 * parts :]
    count, cols = old.shape
    waves = turned.shape[1]
    core = lax.axis_index("col")
    at = 0
    for piece, mine in zip(pieces, owns):
        place = slice(at, at + piece.shape[1])
        at = place.stop
        older = piece[...]
        old[:, place] = jnp.where(lax.axis_index("tm") > 0, older, jnp.zeros_like(older))
        if parts > 1:
            own[:, place] = mine[...]
    if parts == 1:
        own = owns[0]
    total = jnp.dot(table[...], old[...], preferred_element_type=F32)
    total = (total + spec[:, lo : lo + cols]) * gain[...]
    index = lax.broadcasted_iota(jnp.int32, (waves, 1), 0)
    k = index // rows % BAND_FREQS + 1
    flip = jnp.where(k % 2 == 0, 1.0, -1.0)
    ring = cycle[:, lo : lo + cols]

    def damp(half, source, target):
        scaled = (total if half == 0 else total * flip).astype(BF16)
        for r in range(0, count, 512):
            low = jnp.dot(turned[r : r + 512, :], scaled, preferred_element_type=F32)
            rest = source[r : r + 512, :].astype(F32) - low
            rest = rest.reshape(64, 8, cols) - ring[None]
            target[r : r + 512, :] = rest.reshape(512, cols).astype(BF16)

    def both(sent, kept, source, held):
        damp(sent, source, send)
        if late:
            keep[...] = (total if kept == 0 else total * flip).astype(BF16)
        else:
            damp(kept, held, keep)

    @pl.when(core == 0)
    def _():
        both(1, 0, own, old)

    @pl.when(core != 0)
    def _():
        both(0, 1, old, own)


def hold_kernel(lo, piece, own, scaled, turned, cycle, keep):
    count, cols = own.shape
    ring = cycle[:, lo : lo + cols]

    def damp(source):
        for r in range(0, count, 512):
            low = jnp.dot(turned[r : r + 512, :], scaled[...], preferred_element_type=F32)
            rest = source(slice(r, r + 512)).astype(F32) - low
            rest = rest.reshape(64, 8, cols) - ring[None]
            keep[r : r + 512, :] = rest.reshape(512, cols).astype(BF16)

    @pl.when(lax.axis_index("col") == 0)
    def _():
        here = lax.axis_index("tm") > 0
        damp(lambda r: jnp.where(here, piece[r, :], jnp.zeros((512, cols), BF16)))

    @pl.when(lax.axis_index("col") != 0)
    def _():
        damp(lambda r: own[r, :])


def filter_kernel(starts, first, last, rows, *refs):
    n = len(starts)
    taps = refs[n]
    acc = None if first else refs[n + 1]
    if last:
        out, buffer, sems = refs[-3:]
    else:
        out = refs[-1]
    width = out.shape[-1]
    count = refs[0].shape[0]
    step = count // FINISH if last else 256

    depth = refs[0].shape[1]
    offs = [(-start) % width for start in starts]
    if n * depth <= TAP_ROWS:
        weights = [jnp.concatenate([taps[:depth, o : o + width] for o in offs], axis=0)]
    else:
        weights = [taps[:depth, o : o + width] for o in offs]

    def block(r):
        total = None if first else acc[r, :]
        data = [ref[r, :] for ref in refs[:n]]
        if len(weights) == 1:
            data = [jnp.concatenate(data, axis=1)]
        for x, w in zip(data, weights):
            part = jnp.dot(x, w, preferred_element_type=F32)
            total = part if total is None else total + part
        return total

    if last:
        copies = []
        for i in range(FINISH):
            part = pl.ds(i * (step // rows), step // rows)
            total = block(slice(i * step, (i + 1) * step)).astype(BF16)
            buffer[part] = total.reshape(step // rows, rows, width)
            copies.append(pltpu.make_async_copy(buffer.at[part], out.at[part], sems.at[i]))
            copies[-1].start()
        for copy in copies:
            copy.wait()
    else:
        for b in range(0, count, step):
            out[b : b + step, :] = block(slice(b, b + step))


def tap_kernel(shift, out):
    width = out.shape[1] // 2
    lanes = 128
    for r in range(0, lanes, 16):
        row = lax.broadcasted_iota(jnp.int32, (16, width), 0) + r
        col = lax.broadcasted_iota(jnp.int32, (16, width), 1)
        lag = col - row - shift[0]
        lag = jnp.where(lag < 0, lag + width, lag)
        lag = jnp.where(lag < 0, lag + width, lag)
        near = jnp.minimum(lag, width - lag)
        size = jnp.maximum(near, 1).astype(F32)
        odd = -1.0 / (math.pi**2 * size**2)
        tap = jnp.where(near == 0, 0.25, jnp.where((near & 1) == 1, odd, 0.0)).astype(BF16)
        for b in range(out.shape[0] // lanes):
            for c in range(0, 2 * width, width):
                start = (c + b * lanes) % (2 * width)
                rows = slice(b * lanes + r, b * lanes + r + 16)
                room = min(width, 2 * width - start)
                out[rows, start : start + room] = tap[:, :room]
                if room < width:
                    out[rows, : width - room] = tap[:, room:]


def along_tm(x, distance, wrap=True):
    tm = lax.axis_size("tm")
    route = [(i, (i + distance) % tm) for i in range(tm if wrap else tm - distance)]
    return lax.ppermute(x, "tm", route)


def tiny(body, shapes, *args):
    def kernel(*refs):
        for ref, value in zip(refs[len(args) :], body(*(r[...] for r in refs[: len(args)]))):
            ref[...] = value

    return pl.pallas_call(
        kernel,
        out_shape=tuple(jax.ShapeDtypeStruct(s, F32) for s in shapes),
        in_specs=[VMEM] * len(args),
        out_specs=(VMEM,) * len(shapes),
        **params(1 << 16, 1 << 16),
    )(*args)


def row_edges(x):
    place = lax.axis_index("cuts")
    if lax.axis_size("cuts") == 2:
        return (jnp.where(place == 0, x[-1:], x[:1]),)
    return x[-1:], x[:1]


def row_neighbours(last, first=None):
    cuts = lax.axis_size("cuts")
    if cuts == 1:
        return last, last
    up = [(i, (i + 1) % cuts) for i in range(cuts)]
    before = lax.ppermute(last, "cuts", up)
    if cuts == 2:
        return before, before
    return before, lax.ppermute(first, "cuts", [(j, i) for i, j in up])


def lag_distances(tm):
    return [1 << i for i in range(max(tm - 1, 1).bit_length())]


def cycle_of(sums, first_lag, scales):
    rows, cols = sums.shape
    wide = (rows, cols)
    distances = lag_distances(lax.axis_size("tm"))
    n = len(distances)
    older, window, got = None, sums, first_lag
    for i, d in enumerate(distances):
        if i > 0:
            got = along_tm(window, d)
        if i == n - 1:
            break

        def extend(c, got, window, older=None, i=i, d=d):
            got = jnp.where(lax.axis_index("tm") >= d, got, 0.0)
            further = got if older is None else older + c[:, i : i + 1] * got
            return further, window + c[:, n + i : n + i + 1] * got

        extra = () if older is None else (older,)
        older, window = tiny(extend, [wide] * 2, scales, got, window, *extra)

    def estimate_of(c, got, whole, older=None):
        got = jnp.where(lax.axis_index("tm") >= distances[-1], got, 0.0)
        total = got if older is None else older + c[:, n - 1 : n] * got
        total = whole + c[:, 2 * n : 2 * n + 1] * total + total
        x = total * c[:, 2 * n + 1 : 2 * n + 2]
        return x, *row_edges(x)

    extra = () if older is None else (older,)
    edge = (1, cols)
    edges = [edge] * (1 if lax.axis_size("cuts") == 2 else 2)
    estimate, *ends = tiny(estimate_of, [wide, *edges], scales, got, sums, *extra)
    before, after = row_neighbours(*ends)
    return pl.pallas_call(
        smooth_kernel,
        out_shape=jax.ShapeDtypeStruct((8, cols), F32),
        in_specs=[VMEM] * 3,
        out_specs=VMEM,
        name="smooth",
        **params(1 << 16, 1 << 16),
    )(estimate, before, after)


def local(turns, shifts, bands, memory):
    half, rows, cols = turns.shape
    angles, count = 2 * half, half * rows
    width = lax.axis_size("col") * cols
    waves = WAVES * rows
    table, turned = (jnp.asarray(t) for t in wave_tables(half, rows))
    core = lax.axis_index("col").astype(jnp.int32)
    distances = lag_distances(lax.axis_size("tm"))
    n = len(PIECES)

    shapes = [jax.ShapeDtypeStruct((count, hi - lo), BF16) for lo, hi in PIECES]
    turns = pltpu.with_memory_space_constraint(turns, pltpu.HBM)
    head = pl.pallas_call(
        head_kernel,
        out_shape=shapes[0],
        in_specs=[ANY],
        out_specs=VMEM,
        scratch_shapes=[
            pltpu.VMEM((half, rows, PIECES[0][1]), BF16),
            pltpu.SemaphoreType.DMA((4,)),
        ],
        name="head",
        **params(count * cols, count * cols),
    )(turns)
    *pieces, sums = pl.pallas_call(
        split_kernel,
        out_shape=(*shapes[1:], jax.ShapeDtypeStruct((rows, cols), F32)),
        in_specs=[ANY],
        out_specs=[VMEM] * n,
        scratch_shapes=[pltpu.VMEM(turns.shape, BF16), pltpu.SemaphoreType.DMA((4,))],
        name="split",
        **params(16 * count * cols, 4 * count * cols),
    )(turns)
    pieces = [head, *pieces]
    spec, gain, scales = pl.pallas_call(
        functools.partial(spec_kernel, rows, distances, angles),
        out_shape=(
            jax.ShapeDtypeStruct((waves, cols), F32),
            jax.ShapeDtypeStruct((waves, 1), F32),
            jax.ShapeDtypeStruct((rows, 128), F32),
        ),
        in_specs=[ANY] * 3 + [VMEM] * n,
        out_specs=[VMEM] * 3,
        scratch_shapes=[
            pltpu.VMEM(table.shape, BF16),
            pltpu.SMEM((rows,), jnp.int32),
            pltpu.SMEM((rows,), F32),
            pltpu.SemaphoreType.DMA((3,)),
        ],
        name="spec",
        **params(2 * waves * count * cols, 4 * count * cols),
    )(*(pltpu.with_memory_space_constraint(x, pltpu.HBM) for x in (bands, memory, table)), *pieces)
    first_lag = along_tm(sums, 1)
    cycle = cycle_of(sums, first_lag, scales)
    olds = []
    for i, x in enumerate(pieces):
        olds.append(along_tm(x, 1, wrap=i in WRAPS))
    offset = (shifts + core.reshape(1) * cols) % width
    taps = pl.pallas_call(
        tap_kernel,
        out_shape=jax.ShapeDtypeStruct((TAP_ROWS, 2 * width), BF16),
        in_specs=[SMEM],
        out_specs=VMEM,
        name="taps",
        **params(1 << 20, 1 << 20),
    )(offset)

    def damp(i):
        stage = STAGES[i]
        lo, hi = PIECES[stage[0]][0], PIECES[stage[-1]][1]
        shape = jax.ShapeDtypeStruct((count, hi - lo), BF16)
        inputs = [olds[j] for j in stage] + [pieces[j] for j in stage]
        inputs += [spec, gain, table, turned, cycle]
        spare = (count, hi - lo) if len(stage) > 1 else (16, 128)
        late = i == len(STAGES) - 1
        held = jax.ShapeDtypeStruct((waves, hi - lo), BF16) if late else shape
        keep, send = pl.pallas_call(
            functools.partial(damp_kernel, lo, rows, len(stage), late),
            out_shape=(held, shape),
            in_specs=[VMEM] * len(inputs),
            out_specs=[VMEM] * 2,
            scratch_shapes=[pltpu.VMEM((count, hi - lo), BF16), pltpu.VMEM(spare, BF16)],
            **params(6 * waves * count * (hi - lo), 8 * count * (hi - lo)),
        )(*inputs)
        recv = lax.ppermute(send, "col", [(0, 1), (1, 0)])
        if late:
            (j,) = stage
            keep = pl.pallas_call(
                functools.partial(hold_kernel, lo),
                out_shape=shape,
                in_specs=[VMEM] * 5,
                out_specs=VMEM,
                name="hold",
                **params(2 * waves * count * (hi - lo), 4 * count * (hi - lo)),
            )(olds[j], pieces[j], keep, turned, cycle)
        return (lo, cols + lo), (keep, recv)

    def accumulate(part, acc, last):
        starts, data = part
        inputs = [*data, taps] + ([] if acc is None else [acc])
        kernel = functools.partial(filter_kernel, starts, acc is None, last, rows)
        depth = sum(x.shape[1] for x in data)
        cost = params(2 * count * depth * width, 8 * count * width, (16 if last else 8) << 20)
        specs = [VMEM] * len(inputs)
        if last:
            return pl.pallas_call(
                kernel,
                out_shape=jax.ShapeDtypeStruct((half, rows, width), BF16),
                in_specs=specs,
                out_specs=ANY,
                scratch_shapes=[
                    pltpu.VMEM((half, rows, width), BF16),
                    pltpu.SemaphoreType.DMA((FINISH,)),
                ],
                name="finish",
                **cost,
            )(*inputs)
        return pl.pallas_call(
            kernel,
            out_shape=jax.ShapeDtypeStruct((count, width), F32),
            in_specs=specs,
            out_specs=VMEM,
            input_output_aliases={} if acc is None else {len(inputs) - 1: 0},
            **cost,
        )(*inputs)

    acc = None
    for i in range(len(STAGES)):
        starts, data = damp(i)
        if i == len(STAGES) - 2:
            acc = accumulate((starts[:1], data[:1]), acc, False)
            acc = accumulate((starts[1:], data[1:]), acc, False)
        else:
            acc = accumulate((starts, data), acc, i == len(STAGES) - 1)
    return acc


def solution(mesh):
    placed = (
        P(("groups", "tm"), "cuts", "col"),
        P(("groups", "tm")),
        P(("groups", "cuts")),
        P(("groups", "cuts")),
    )

    return jax.shard_map(
        local,
        mesh=mesh,
        in_specs=placed,
        out_specs=P(("groups", "tm", "col"), "cuts", None),
        check_vma=False,
    )
```

```python
import functools
import math

import jax
import jax.numpy as jnp
import numpy as np
from jax import lax
from jax.experimental import pallas as pl
from jax.experimental.pallas import tpu as pltpu
from jax.sharding import PartitionSpec as P

BAND_FREQS = 64
WAVES = 2 * BAND_FREQS
TAP_ROWS = 256
FINISH = 4
PIECES = ((0, 128), (128, 256), (256, 512), (512, 640))
STAGES = ((0, 1), (2,), (3,))
WRAPS = (0, 1)

VMEM = pl.BlockSpec(memory_space=pltpu.VMEM)
SMEM = pl.BlockSpec(memory_space=pltpu.SMEM)
ANY = pl.BlockSpec(memory_space=pl.ANY)
F32 = jnp.float32
BF16 = jnp.bfloat16


def wave_tables(half, rows):
    k = np.arange(BAND_FREQS)[:, None] + 1
    m = (k * np.arange(half)[None, :]) % (2 * half)
    phase = m.astype(np.float64) * (2.0 * math.pi / (2 * half))
    waves = np.concatenate([np.cos(phase), np.sin(phase)], axis=0).astype(np.float32)
    eye = np.eye(rows, dtype=np.float32)
    spread = (waves[:, None, :, None] * eye[None, :, None, :]).reshape(WAVES * rows, half * rows)
    return spread.astype(jnp.bfloat16), np.ascontiguousarray(spread.T).astype(jnp.bfloat16)


def params(flops, size, grant=8 << 20):
    return dict(
        compiler_params=pltpu.CompilerParams(vmem_limit_bytes=grant),
        cost_estimate=pl.CostEstimate(flops=flops, bytes_accessed=size, transcendentals=0),
    )


def pattern(shape, dim, rows):
    return lax.broadcasted_iota(jnp.int32, shape, dim) % rows


def fetch(raw, buffer, sems, columns):
    count = sems.shape[0]
    block = raw.shape[0] // count
    parts = [pl.ds(i * block, block) for i in range(count)]
    copies = [
        pltpu.make_async_copy(raw.at[p, :, columns], buffer.at[p], sems.at[i])
        for i, p in enumerate(parts)
    ]
    for copy in copies:
        copy.start()
    return copies


def head_kernel(raw, out, buffer, sems):
    half, rows, cols = buffer.shape
    block = half // sems.shape[0]
    for i, copy in enumerate(fetch(raw, buffer, sems, pl.ds(*PIECES[0]))):
        copy.wait()
        x = buffer[i * block : (i + 1) * block].reshape(block * rows, cols)
        out[i * block * rows : (i + 1) * block * rows, :] = x


def split_kernel(raw, *refs):
    *pieces, sums, buffer, sems = refs
    half, rows, cols = buffer.shape
    block = half // sems.shape[0]
    shape = (8, block * rows)
    pick = pattern(shape, 1, rows) == lax.broadcasted_iota(jnp.int32, shape, 0)
    pick = pick.astype(F32).astype(BF16)
    total = None
    for i, copy in enumerate(fetch(raw, buffer, sems, pl.ds(0, cols))):
        copy.wait()
        x = buffer[i * block : (i + 1) * block].reshape(block * rows, cols)
        for (lo, hi), out in zip(PIECES[1:], pieces):
            out[i * block * rows : (i + 1) * block * rows, :] = x[:, lo:hi]
        part = jnp.dot(pick, x, preferred_element_type=F32)
        total = part if total is None else total + part
    sums[...] = total[:rows, :]


def spec_kernel(rows, distances, angles, bands, memory, table, *refs):
    *pieces, spec, gain, scales, local_table, local_bands, local_memory, sems = refs
    pairs = [(bands, local_bands), (memory, local_memory), (table, local_table)]
    copies = [pltpu.make_async_copy(a, b, sems.at[i]) for i, (a, b) in enumerate(pairs)]
    for copy in copies:
        copy.start()
    for copy in copies:
        copy.wait()
    bands, memory, table = local_bands, local_memory, local_table
    waves = spec.shape[0]
    index = lax.broadcasted_iota(jnp.int32, (waves, 1), 0)
    k = index // rows % BAND_FREQS + 1
    flip = jnp.where(k % 2 == 0, 1.0, -1.0)
    for (lo, hi), piece in zip(PIECES, pieces):
        spec[:, lo:hi] = flip * jnp.dot(table[...], piece[...], preferred_element_type=F32)
    band = jnp.full((waves, 1), bands[0], jnp.int32)
    row = lax.broadcasted_iota(jnp.int32, (rows, 1), 0)
    decay = jnp.full((rows, 1), memory[0], F32)
    for s in range(1, rows):
        band = jnp.where(index % rows == s, bands[s], band)
        decay = jnp.where(row == s, memory[s], decay)
    square = (k * k).astype(F32)
    gain[...] = jnp.exp(-square / (2.0 * (band * band).astype(F32))) * (2.0 / angles)
    power, done = decay, 1
    for i, d in enumerate(distances):
        while done < d:
            power, done = power * power, 2 * done
        scales[:, i : i + 1] = jnp.ones_like(decay) if d == 1 else power / decay
        scales[:, len(distances) + i : len(distances) + i + 1] = power
    weight = jnp.ones_like(decay)
    steps = lax.axis_index("tm")
    for j in range(lax.axis_size("tm") - 1):
        weight = jnp.where(j < steps, weight * decay + 1.0, weight)
    scales[:, 2 * len(distances) : 2 * len(distances) + 1] = decay
    scales[:, 2 * len(distances) + 1 : 2 * len(distances) + 2] = 1.0 / (weight * angles)


def smooth_kernel(estimate, before, after, out):
    rows, cols = estimate.shape
    x = estimate[...]
    place = lax.axis_index("cuts")
    first = jnp.where(place != 0, before[...], 0.0)
    last = jnp.where(place != lax.axis_size("cuts") - 1, after[...], 0.0)
    up = jnp.concatenate([first, x[:-1]], axis=0)
    down = jnp.concatenate([x[1:], last], axis=0)
    ring = (up + 2.0 * x + down) * 0.25
    row = pattern((8, cols), 0, rows)
    total = jnp.broadcast_to(ring[:1], (8, cols))
    for s in range(1, rows):
        total = jnp.where(row == s, jnp.broadcast_to(ring[s : s + 1], (8, cols)), total)
    out[...] = total


def damp_kernel(lo, rows, parts, late, *refs):
    pieces, owns = refs[:parts], refs[parts : 2 * parts]
    spec, gain, table, turned, cycle, keep, send, old, own = refs[2 * parts :]
    count, cols = old.shape
    waves = turned.shape[1]
    core = lax.axis_index("col")
    at = 0
    for piece, mine in zip(pieces, owns):
        place = slice(at, at + piece.shape[1])
        at = place.stop
        older = piece[...]
        old[:, place] = jnp.where(lax.axis_index("tm") > 0, older, jnp.zeros_like(older))
        if parts > 1:
            own[:, place] = mine[...]
    if parts == 1:
        own = owns[0]
    total = jnp.dot(table[...], old[...], preferred_element_type=F32)
    total = (total + spec[:, lo : lo + cols]) * gain[...]
    index = lax.broadcasted_iota(jnp.int32, (waves, 1), 0)
    k = index // rows % BAND_FREQS + 1
    flip = jnp.where(k % 2 == 0, 1.0, -1.0)
    ring = cycle[:, lo : lo + cols]

    def damp(half, source, target):
        scaled = (total if half == 0 else total * flip).astype(BF16)
        for r in range(0, count, 256):
            low = jnp.dot(turned[r : r + 256, :], scaled, preferred_element_type=F32)
            rest = source[r : r + 256, :].astype(F32) - low
            rest = rest.reshape(32, 8, cols) - ring[None]
            target[r : r + 256, :] = rest.reshape(256, cols).astype(BF16)

    def both(sent, kept, source, held):
        damp(sent, source, send)
        if late:
            keep[...] = (total if kept == 0 else total * flip).astype(BF16)
        else:
            damp(kept, held, keep)

    @pl.when(core == 0)
    def _():
        both(1, 0, own, old)

    @pl.when(core != 0)
    def _():
        both(0, 1, old, own)


def hold_kernel(lo, piece, own, scaled, turned, cycle, keep):
    count, cols = own.shape
    ring = cycle[:, lo : lo + cols]

    def damp(source):
        for r in range(0, count, 256):
            low = jnp.dot(turned[r : r + 256, :], scaled[...], preferred_element_type=F32)
            rest = source(slice(r, r + 256)).astype(F32) - low
            rest = rest.reshape(32, 8, cols) - ring[None]
            keep[r : r + 256, :] = rest.reshape(256, cols).astype(BF16)

    @pl.when(lax.axis_index("col") == 0)
    def _():
        here = lax.axis_index("tm") > 0
        damp(lambda r: jnp.where(here, piece[r, :], jnp.zeros((256, cols), BF16)))

    @pl.when(lax.axis_index("col") != 0)
    def _():
        damp(lambda r: own[r, :])


def filter_kernel(starts, first, last, rows, *refs):
    n = len(starts)
    taps = refs[n]
    acc = None if first else refs[n + 1]
    if last:
        out, buffer, sems = refs[-3:]
    else:
        out = refs[-1]
    width = out.shape[-1]
    count = refs[0].shape[0]
    step = count // FINISH if last else 512

    depth = refs[0].shape[1]
    offs = [(-start) % width for start in starts]
    if n * depth <= TAP_ROWS:
        weights = [jnp.concatenate([taps[:depth, o : o + width] for o in offs], axis=0)]
    else:
        weights = [taps[:depth, o : o + width] for o in offs]

    def block(r):
        total = None if first else acc[r, :]
        data = [ref[r, :] for ref in refs[:n]]
        if len(weights) == 1:
            data = [jnp.concatenate(data, axis=1)]
        for x, w in zip(data, weights):
            part = jnp.dot(x, w, preferred_element_type=F32)
            total = part if total is None else total + part
        return total

    if last:
        copies = []
        for i in range(FINISH):
            part = pl.ds(i * (step // rows), step // rows)
            total = block(slice(i * step, (i + 1) * step)).astype(BF16)
            buffer[part] = total.reshape(step // rows, rows, width)
            copies.append(pltpu.make_async_copy(buffer.at[part], out.at[part], sems.at[i]))
            copies[-1].start()
        for copy in copies:
            copy.wait()
    else:
        for b in range(0, count, step):
            out[b : b + step, :] = block(slice(b, b + step))


def tap_kernel(shift, out):
    width = out.shape[1] // 2
    lanes = 128
    for r in range(0, lanes, 16):
        row = lax.broadcasted_iota(jnp.int32, (16, width), 0) + r
        col = lax.broadcasted_iota(jnp.int32, (16, width), 1)
        lag = col - row - shift[0]
        lag = jnp.where(lag < 0, lag + width, lag)
        lag = jnp.where(lag < 0, lag + width, lag)
        near = jnp.minimum(lag, width - lag)
        size = jnp.maximum(near, 1).astype(F32)
        odd = -1.0 / (math.pi**2 * size**2)
        tap = jnp.where(near == 0, 0.25, jnp.where((near & 1) == 1, odd, 0.0)).astype(BF16)
        for b in range(out.shape[0] // lanes):
            for c in range(0, 2 * width, width):
                start = (c + b * lanes) % (2 * width)
                rows = slice(b * lanes + r, b * lanes + r + 16)
                room = min(width, 2 * width - start)
                out[rows, start : start + room] = tap[:, :room]
                if room < width:
                    out[rows, : width - room] = tap[:, room:]


def along_tm(x, distance, wrap=True):
    tm = lax.axis_size("tm")
    route = [(i, (i + distance) % tm) for i in range(tm if wrap else tm - distance)]
    return lax.ppermute(x, "tm", route)


def tiny(body, shapes, *args):
    def kernel(*refs):
        for ref, value in zip(refs[len(args) :], body(*(r[...] for r in refs[: len(args)]))):
            ref[...] = value

    return pl.pallas_call(
        kernel,
        out_shape=tuple(jax.ShapeDtypeStruct(s, F32) for s in shapes),
        in_specs=[VMEM] * len(args),
        out_specs=(VMEM,) * len(shapes),
        **params(1 << 16, 1 << 16),
    )(*args)


def row_edges(x):
    place = lax.axis_index("cuts")
    if lax.axis_size("cuts") == 2:
        return (jnp.where(place == 0, x[-1:], x[:1]),)
    return x[-1:], x[:1]


def row_neighbours(last, first=None):
    cuts = lax.axis_size("cuts")
    if cuts == 1:
        return last, last
    up = [(i, (i + 1) % cuts) for i in range(cuts)]
    before = lax.ppermute(last, "cuts", up)
    if cuts == 2:
        return before, before
    return before, lax.ppermute(first, "cuts", [(j, i) for i, j in up])


def lag_distances(tm):
    return [1 << i for i in range(max(tm - 1, 1).bit_length())]


def cycle_of(sums, first_lag, scales):
    rows, cols = sums.shape
    wide = (rows, cols)
    distances = lag_distances(lax.axis_size("tm"))
    n = len(distances)
    older, window, got = None, sums, first_lag
    for i, d in enumerate(distances):
        if i > 0:
            got = along_tm(window, d)
        if i == n - 1:
            break

        def extend(c, got, window, older=None, i=i, d=d):
            got = jnp.where(lax.axis_index("tm") >= d, got, 0.0)
            further = got if older is None else older + c[:, i : i + 1] * got
            return further, window + c[:, n + i : n + i + 1] * got

        extra = () if older is None else (older,)
        older, window = tiny(extend, [wide] * 2, scales, got, window, *extra)

    def estimate_of(c, got, whole, older=None):
        got = jnp.where(lax.axis_index("tm") >= distances[-1], got, 0.0)
        total = got if older is None else older + c[:, n - 1 : n] * got
        total = whole + c[:, 2 * n : 2 * n + 1] * total + total
        x = total * c[:, 2 * n + 1 : 2 * n + 2]
        return x, *row_edges(x)

    extra = () if older is None else (older,)
    edge = (1, cols)
    edges = [edge] * (1 if lax.axis_size("cuts") == 2 else 2)
    estimate, *ends = tiny(estimate_of, [wide, *edges], scales, got, sums, *extra)
    before, after = row_neighbours(*ends)
    return pl.pallas_call(
        smooth_kernel,
        out_shape=jax.ShapeDtypeStruct((8, cols), F32),
        in_specs=[VMEM] * 3,
        out_specs=VMEM,
        name="smooth",
        **params(1 << 16, 1 << 16),
    )(estimate, before, after)


def local(turns, shifts, bands, memory):
    half, rows, cols = turns.shape
    angles, count = 2 * half, half * rows
    width = lax.axis_size("col") * cols
    waves = WAVES * rows
    table, turned = (jnp.asarray(t) for t in wave_tables(half, rows))
    core = lax.axis_index("col").astype(jnp.int32)
    distances = lag_distances(lax.axis_size("tm"))
    n = len(PIECES)

    shapes = [jax.ShapeDtypeStruct((count, hi - lo), BF16) for lo, hi in PIECES]
    turns = pltpu.with_memory_space_constraint(turns, pltpu.HBM)
    head = pl.pallas_call(
        head_kernel,
        out_shape=shapes[0],
        in_specs=[ANY],
        out_specs=VMEM,
        scratch_shapes=[
            pltpu.VMEM((half, rows, PIECES[0][1]), BF16),
            pltpu.SemaphoreType.DMA((4,)),
        ],
        name="head",
        **params(count * cols, count * cols),
    )(turns)
    *pieces, sums = pl.pallas_call(
        split_kernel,
        out_shape=(*shapes[1:], jax.ShapeDtypeStruct((rows, cols), F32)),
        in_specs=[ANY],
        out_specs=[VMEM] * n,
        scratch_shapes=[pltpu.VMEM(turns.shape, BF16), pltpu.SemaphoreType.DMA((4,))],
        name="split",
        **params(16 * count * cols, 4 * count * cols),
    )(turns)
    pieces = [head, *pieces]
    spec, gain, scales = pl.pallas_call(
        functools.partial(spec_kernel, rows, distances, angles),
        out_shape=(
            jax.ShapeDtypeStruct((waves, cols), F32),
            jax.ShapeDtypeStruct((waves, 1), F32),
            jax.ShapeDtypeStruct((rows, 128), F32),
        ),
        in_specs=[ANY] * 3 + [VMEM] * n,
        out_specs=[VMEM] * 3,
        scratch_shapes=[
            pltpu.VMEM(table.shape, BF16),
            pltpu.SMEM((rows,), jnp.int32),
            pltpu.SMEM((rows,), F32),
            pltpu.SemaphoreType.DMA((3,)),
        ],
        name="spec",
        **params(2 * waves * count * cols, 4 * count * cols),
    )(*(pltpu.with_memory_space_constraint(x, pltpu.HBM) for x in (bands, memory, table)), *pieces)
    first_lag = along_tm(sums, 1)
    cycle = cycle_of(sums, first_lag, scales)
    olds = []
    for i, x in enumerate(pieces):
        olds.append(along_tm(x, 1, wrap=i in WRAPS))
    offset = (shifts + core.reshape(1) * cols) % width
    taps = pl.pallas_call(
        tap_kernel,
        out_shape=jax.ShapeDtypeStruct((TAP_ROWS, 2 * width), BF16),
        in_specs=[SMEM],
        out_specs=VMEM,
        name="taps",
        **params(1 << 20, 1 << 20),
    )(offset)

    def damp(i):
        stage = STAGES[i]
        lo, hi = PIECES[stage[0]][0], PIECES[stage[-1]][1]
        shape = jax.ShapeDtypeStruct((count, hi - lo), BF16)
        inputs = [olds[j] for j in stage] + [pieces[j] for j in stage]
        inputs += [spec, gain, table, turned, cycle]
        spare = (count, hi - lo) if len(stage) > 1 else (16, 128)
        late = i == len(STAGES) - 1
        held = jax.ShapeDtypeStruct((waves, hi - lo), BF16) if late else shape
        keep, send = pl.pallas_call(
            functools.partial(damp_kernel, lo, rows, len(stage), late),
            out_shape=(held, shape),
            in_specs=[VMEM] * len(inputs),
            out_specs=[VMEM] * 2,
            scratch_shapes=[pltpu.VMEM((count, hi - lo), BF16), pltpu.VMEM(spare, BF16)],
            **params(6 * waves * count * (hi - lo), 8 * count * (hi - lo)),
        )(*inputs)
        recv = lax.ppermute(send, "col", [(0, 1), (1, 0)])
        if late:
            (j,) = stage
            keep = pl.pallas_call(
                functools.partial(hold_kernel, lo),
                out_shape=shape,
                in_specs=[VMEM] * 5,
                out_specs=VMEM,
                name="hold",
                **params(2 * waves * count * (hi - lo), 4 * count * (hi - lo)),
            )(olds[j], pieces[j], keep, turned, cycle)
        return (lo, cols + lo), (keep, recv)

    def accumulate(part, acc, last):
        starts, data = part
        inputs = [*data, taps] + ([] if acc is None else [acc])
        kernel = functools.partial(filter_kernel, starts, acc is None, last, rows)
        depth = sum(x.shape[1] for x in data)
        cost = params(2 * count * depth * width, 8 * count * width, (16 if last else 8) << 20)
        specs = [VMEM] * len(inputs)
        if last:
            return pl.pallas_call(
                kernel,
                out_shape=jax.ShapeDtypeStruct((half, rows, width), BF16),
                in_specs=specs,
                out_specs=ANY,
                scratch_shapes=[
                    pltpu.VMEM((half, rows, width), BF16),
                    pltpu.SemaphoreType.DMA((FINISH,)),
                ],
                name="finish",
                **cost,
            )(*inputs)
        return pl.pallas_call(
            kernel,
            out_shape=jax.ShapeDtypeStruct((count, width), F32),
            in_specs=specs,
            out_specs=VMEM,
            input_output_aliases={} if acc is None else {len(inputs) - 1: 0},
            **cost,
        )(*inputs)

    acc = None
    for i in range(len(STAGES)):
        starts, data = damp(i)
        if i == len(STAGES) - 2:
            acc = accumulate((starts[:1], data[:1]), acc, False)
            acc = accumulate((starts[1:], data[1:]), acc, False)
        else:
            acc = accumulate((starts, data), acc, i == len(STAGES) - 1)
    return acc


def solution(mesh):
    placed = (
        P(("groups", "tm"), "cuts", "col"),
        P(("groups", "tm")),
        P(("groups", "cuts")),
        P(("groups", "cuts")),
    )

    return jax.shard_map(
        local,
        mesh=mesh,
        in_specs=placed,
        out_specs=P(("groups", "tm", "col"), "cuts", None),
        check_vma=False,
    )
```
